256 devices in a mesh: gx: 16 (over x, z_lo, core), gy: 16 (over y, z_hi).
Axes of the slice: x: 4, y: 4, z: 8 (z_hi: 4, z_lo: 2; z = z_hi * 2 + z_lo), core: 2. Of those that a mesh axis runs over, the one named last changes fastest.
Arguments:
- stem_first: float32 [16, 2048, 1024], P('gx', 'gy'), may hold values from -6 to 6
- cotangent: float32 [16, 2048, 1024], P('gx', 'gy'), may hold values from -6 to 6
- branch_first: float32 [1024, 1024], P(('gx', 'gy')), may hold values from -0.1875 to 0.1875
- branch_second: float32 [1024, 1024], P(('gx', 'gy')), may hold values from -0.1875 to 0.1875
- bond_first: int32 [1024], replicated, may hold values from 0 to 1023, each once
- bond_second: int32 [1024], replicated, may hold values from 0 to 1023, each once
Outputs:
- grad_stem: float32 [16, 2048, 1024], P('gx', 'gy')
- grad_first: float32 [1024, 1024], P(('gx', 'gy'))
- grad_second: float32 [1024, 1024], P(('gx', 'gy'))
The draws below stay inside these ranges and needn't reach their ends.
Inputs may be any that keep to these rules, and one draw needn't show every extreme that they name: `bond_first`: each a permutation of the numbers below 1024. `bond_second`: each a permutation of the numbers below 1024.
All inputs are finite; a program needn't handle non-finite values.
Results may differ from the reference program's by a relative error of at most 0.000098.
Values sent between devices are 32-bit elements; how exact they have to be, the bound alone decides.
A program may use at most 64 MiB of HBM per device.

```python
import jax
import jax.numpy as jnp
from jax import lax

BOND = 1024
ROWS = 2048
N_GX = 16


def spiked(entries, rng, source, target, shards_of, factor):
    owner, partner = [(jnp.arange(entries.shape[axis_at]) // (entries.shape[axis_at] // shards_of)).reshape([-1 if axis == axis_at else 1 for axis in range(entries.ndim)]) for axis_at in (source, target)]
    chosen = jax.random.permutation(rng, shards_of)[partner]
    strong = (owner == chosen) | (owner == (partner + shards_of // 2) % shards_of)
    return jnp.where(strong, factor * entries, entries)


def levels(key, extent, pieces, least, largest):
    def one(dim, blocks):
        draws = jax.random.uniform(jax.random.fold_in(jax.random.fold_in(key, 6), dim), (blocks,), jnp.float32, least / len(pieces), largest / len(pieces))
        return jnp.repeat(jnp.exp(draws), extent[dim] // blocks).reshape((-1,) + (1,) * (len(extent) - dim - 1))

    level = one(*pieces[0])
    for cut in pieces[1:]:
        level = level * one(*cut)
    return level


def centred(stream_key, dims, scale, most, cuts=(), held_as=jnp.bfloat16):
    factor_of = levels(stream_key, dims, cuts, -0.22, 0.18) if cuts else 1.0
    values = jax.random.normal(stream_key, dims, jnp.float32) * scale * factor_of
    return jnp.minimum(jnp.maximum(values, -most), most).astype(held_as)


def gaussian_with(key, shape, spread, reach, cuts, heavy, kind=jnp.bfloat16):
    values = spread * jax.random.normal(key, shape, jnp.float32)
    if cuts:
        values = values * levels(key, shape, cuts, -0.22, 0.18)
    return jnp.clip(spiked(values, jax.random.fold_in(key, 3), *heavy), -reach, reach).astype(kind)


def setup_inputs(seed: int = 0) -> dict:
    key_list = jax.random.split(jax.random.key(seed), 7)
    stem_first = gaussian_with(key_list[0], (N_GX, ROWS, BOND), 1.0, 6.0, ((0, 16), (1, 16)), (1, 2, 16, 2.0), jnp.float32)
    cotangent = centred(key_list[1], (N_GX, ROWS, BOND), 1.0, 6.0, ((0, 16), (1, 16)), jnp.float32)
    branch_first = centred(key_list[2], (BOND, BOND), BOND ** -0.5, 0.1875, ((0, 256),), jnp.float32)
    branch_second = centred(key_list[3], (BOND, BOND), BOND ** -0.5, 0.1875, ((0, 256),), jnp.float32)
    bond_first = jax.random.permutation(key_list[4], BOND).astype(jnp.int32)
    bond_second = jax.random.permutation(key_list[5], BOND).astype(jnp.int32)
    return dict(stem_first=stem_first, cotangent=cotangent, branch_first=branch_first, branch_second=branch_second, bond_first=bond_first, bond_second=bond_second)


def inverse(ordering):
    return jnp.zeros_like(ordering).at[ordering].set(jnp.arange(ordering.shape[0], dtype=jnp.int32))

def product(left, right):
    return jnp.dot(left, right, precision=lax.Precision.HIGHEST, preferred_element_type=jnp.float32)

def regroup(field):
    groups, height, width = field.shape
    blocks = field.reshape(groups, height, groups, width // groups)
    return jnp.transpose(blocks, (2, 1, 0, 3)).reshape(groups, height, width)

def reference(stem_first, cotangent, branch_first, branch_second, bond_first, bond_second):
    groups, height, width = stem_first.shape
    factor = 1.0 / jnp.sqrt(jnp.float32(groups * height))
    placed_first = branch_first[inverse(bond_first)]
    placed_second = branch_second[inverse(bond_second)]
    stem_flat = stem_first.reshape(groups * height, width)
    cotan_flat = cotangent.reshape(groups * height, width)
    stem_mid = product(stem_flat, placed_first).reshape(groups, height, width)
    regrouped = regroup(stem_mid).reshape(groups * height, width)
    back_regrouped = product(cotan_flat, placed_second.T).reshape(groups, height, width)
    grad_second = product(regrouped[:, bond_second].T, cotan_flat) * factor
    back_mid = regroup(back_regrouped).reshape(groups * height, width)
    grad_first = product(stem_flat[:, bond_first].T, back_mid) * factor
    grad_stem = product(back_mid, placed_first.T).reshape(groups, height, width)
    return (grad_stem, grad_first, grad_second)
```

```python
import jax
import jax.numpy as jnp
from jax import lax
from jax.experimental import pallas as pl
from jax.experimental.pallas import tpu as pltpu
from jax.sharding import PartitionSpec as P

MESH = pl.DeviceIdType.MESH
SIZE = {"x": 4, "y": 4, "z": 8}
AXES = ("x", "y", "z")
ROWS = 128
WIDTH = 1024
HALF = 512
F32 = jnp.float32
BF16 = jnp.bfloat16

STREAMS_A = ((0, 2, "zyx"), (2, 1, "zxy"), (3, 1, "xyz"))
STREAMS_B = ((0, 1, "zyx"), (1, 2, "zxy"), (3, 1, "xyz"))


def dot(left, right, over):
    return lax.dot_general(left, right, (over, ((), ())), preferred_element_type=F32)


def nn(left, right):
    return dot(left, right, ((1,), (0,)))


def nt(left, right):
    return dot(left, right, ((1,), (1,)))


def tn(left, right):
    return dot(left, right, ((0,), (0,)))


def three(form, lhi, llo, rhi, rlo):
    return form(lhi, rhi) + (form(lhi, rlo) + form(llo, rhi))


def parts(value):
    high = value.astype(BF16)
    return high, (value - high.astype(F32)).astype(BF16)


class Place:
    def __init__(self, send, recv):
        gx, gy = lax.axis_index("gx"), lax.axis_index("gy")
        self.core = lax.rem(gx, 2)
        self.low = lax.rem(gx // 2, 2)
        self.at = {"x": gx // 4, "y": gy // 4, "z": lax.rem(gy, 4) * 2 + self.low}
        self.chip = gx // 2
        self.send, self.recv = send, recv
        self.used = 0
        self.open = []

    def device(self, core=None, **where):
        spot = {**self.at, **where}
        core = self.core if core is None else core
        gx = (spot["x"] * 2 + lax.rem(spot["z"], 2)) * 2 + core
        return gx, spot["y"] * 4 + spot["z"] // 2

    def step(self, axis, by):
        return lax.rem(self.at[axis] + (by + SIZE[axis]), SIZE[axis])

    def neighbour(self, axis, sign):
        return self.device(**{axis: self.step(axis, sign)})

    def partner(self):
        return self.device(core=1 - self.core)

    def copy(self, src, dst, device, lands=None):
        slot = self.used
        self.used += 1
        out = pltpu.make_async_remote_copy(
            src_ref=src,
            dst_ref=dst,
            send_sem=self.send.at[slot],
            recv_sem=self.recv.at[slot],
            device_id=device,
            device_id_type=MESH,
        )
        out.start()
        self.open.append(out)
        lands = dst if lands is None else lands
        return pltpu.make_async_remote_copy(
            src_ref=lands,
            dst_ref=lands,
            send_sem=self.send.at[slot],
            recv_sem=self.recv.at[slot],
            device_id=device,
            device_id_type=MESH,
        ).wait_recv

    def close(self):
        for out in self.open:
            out.wait_send()


def view(block, count, spot, cut=None):
    index = [slice(block, block + count)]
    for axis in AXES:
        index.append(pl.ds(spot[axis], 1) if axis in spot else slice(None))
    if cut is not None:
        name, which = cut
        if name == "block":
            index[0] = slice(block + which, block + which + 1)
        else:
            size = SIZE[name] // 2
            index[1 + AXES.index(name)] = slice(which * size, (which + 1) * size)
    return tuple(index) + (slice(None), slice(None))


def cut_of(count, whole):
    return whole[0] if whole else ("block" if count == 2 else None)


def gather(place, buffer, block, count, order):
    whole, waits = [], {}
    for axis in order:
        half = SIZE[axis] // 2
        for tick in range(half):
            if tick == 0:
                for wait in waits.values():
                    wait()
                waits = {}
            fresh = {}
            last = tick == half - 1
            name = cut_of(count, whole) if last else None
            for sign in (1, -1):
                if sign in waits:
                    waits[sign]()
                if last and name is None and sign == -1:
                    continue
                cut = (name, 0 if sign == 1 else 1) if last and name else None
                rest = {a: place.at[a] for a in AXES if a not in whole and a != axis}
                out = buffer.at[view(block, count, {**rest, axis: place.step(axis, -sign * tick)}, cut)]
                lands = buffer.at[view(block, count, {**rest, axis: place.step(axis, -sign * (tick + 1))}, cut)]
                fresh[sign] = place.copy(out, out, place.neighbour(axis, sign), lands)
            waits = fresh
            yield
        whole.append(axis)
    for wait in waits.values():
        wait()
    yield


def landing_shapes(count, order):
    shapes = []
    done = []
    for axis in order[::-1]:
        dims = [1 if a == axis or a in done else SIZE[a] for a in AXES]
        shapes.append((SIZE[axis], count, *dims, 8, 128))
        done.append(axis)
    return shapes


def scatter(place, buffer, landings, block, count, order):
    done = []
    for axis, landing in zip(order[::-1], landings):
        half = SIZE[axis] // 2
        whole = [a for a in AXES if a not in done and a != axis]
        fixed = {a: place.at[a] for a in done}
        name = cut_of(count, whole)
        arriving = {}

        def into(slot, cut):
            return landing.at[(slot, *view(0, count, {}, cut))]

        def add(sign, distance):
            wait, slot, cut = arriving.pop(sign)
            wait()
            where = view(block, count, {**fixed, axis: place.step(axis, sign * distance)}, cut)
            buffer[where] = buffer[where] + into(slot, cut)[...]

        for tick in range(half):
            distance = half - tick
            for place_sign, sign in enumerate((1, -1)):
                if tick == 0 and name is None and sign == -1:
                    continue
                if sign in arriving:
                    add(sign, distance)
                cut = (name, place_sign) if tick == 0 and name else None
                slot = 2 * tick + place_sign
                out = buffer.at[view(block, count, {**fixed, axis: place.step(axis, sign * distance)}, cut)]
                wait = place.copy(out, into(slot, cut), place.neighbour(axis, sign))
                arriving[sign] = (wait, slot, cut)
            yield

        add(1, 0)
        add(-1, 0)
        done.append(axis)
    yield


def run(streams, ticks=1):
    for _ in range(ticks):
        for stream in streams:
            next(stream)


def kernel(
    stem_in, cotan_in, first_in, second_in, bond_q, bond2_q, bond2_z,
    grad_stem, grad_first, grad_second,
    *scratch,
):
    scratch = list(scratch)

    def take(n=None):
        if n is None:
            return scratch.pop(0)
        return [scratch.pop(0) for _ in range(n)]

    send, recv = take(2)
    g1, g2, rx1, stem_rx, cotan_rx = take(5)
    hot1, hot2q, hot2z = take(3)
    p1h, p1l, ch, cl, b1h, b1l, b2h, b2l = take(8)
    z_own, z_out, z_rx = take(3)
    back, back_rx, mid, mid_rx = take(4)
    bmh, bml, sph, spl = take(4)
    y_own, y_out, y_rx, a2_own, a2_rx = take(5)
    s1, s2 = take(2)
    land1 = [take(3) for _ in STREAMS_A]
    land2 = [take(3) for _ in STREAMS_B]

    place = Place(send, recv)
    core = place.core
    mine = core == 0

    barrier = pltpu.get_barrier_semaphore()
    peers = [place.partner(), place.neighbour("y", 1), place.neighbour("y", -1)]
    peers.append(place.neighbour("z", 2 * place.low - 1))
    chips = []
    for hop in range(1, 8):
        chip = lax.rem(place.chip + hop, 8)
        chips.append((chip, (chip * 2 + core, lax.axis_index("gy"))))
    peers += [device for _, device in chips]
    for peer in peers:
        pl.semaphore_signal(barrier, inc=1, device_id=peer, device_id_type=MESH)
    pl.semaphore_wait(barrier, len(peers))

    partner = place.partner()
    first_wait = place.copy(first_in.at[1 - core], rx1, partner)
    here = view(0, 4, place.at)
    g2[here] = second_in[...]
    gathers2 = [gather(place, g2, *s) for s in STREAMS_A]
    run(gathers2)
    first_wait()
    g1[here] = (first_in[core] + rx1[...])
    gathers1 = [gather(place, g1, *s) for s in STREAMS_B]
    run(gathers1)
    stem_wait = place.copy(stem_in, stem_rx, partner)
    cotan_wait = place.copy(cotan_in, cotan_rx, partner)

    def build(hot, row):
        def body(i, _):
            at = pl.multiple_of(i * 64, 64)
            rows = lax.broadcasted_iota(jnp.int32, (64, WIDTH), 0) + at
            hot[pl.ds(at, 64), :] = jnp.where(rows == row[...], 1.0, 0.0).astype(BF16)
            return 0

        lax.fori_loop(0, WIDTH // 64, body, 0)

    def split_rows(src, high, low, base):
        def body(i, _):
            at = pl.multiple_of(i * 32, 32)
            h, l = parts(src[pl.ds(at, 32), :])
            high[pl.ds(base + at, 32), :] = h
            low[pl.ds(base + at, 32), :] = l
            return 0

        lax.fori_loop(0, src.shape[0] // 32, body, 0)

    build(hot1, bond_q)
    run(gathers2)
    run(gathers1)
    split_rows(stem_in, sph, spl, 0)
    stem_wait()
    split_rows(stem_rx, sph, spl, ROWS)
    run(gathers2)
    run(gathers1)

    def permute_stem(i, _):
        at = pl.multiple_of(i * 256, 256)
        hot = hot1[:, pl.ds(at, 256)]
        p1h[:, pl.ds(at, 256)] = nn(sph[...], hot).astype(BF16)
        p1l[:, pl.ds(at, 256)] = nn(spl[...], hot).astype(BF16)
        return 0

    lax.fori_loop(0, 4, permute_stem, 0)
    run(gathers2)
    run(gathers1)
    split_rows(cotan_in, ch, cl, 0)
    cotan_wait()
    split_rows(cotan_rx, ch, cl, ROWS)
    run(gathers2)
    run(gathers1)
    build(hot2z, bond2_z)
    run(gathers2)
    run(gathers1)
    build(hot2q, bond2_q)
    run(gathers2)
    run(gathers1)
    run(gathers2)
    run(gathers1)

    run(gathers2)
    rows8 = lax.broadcasted_iota(jnp.int32, (16, 8, 128), 1)

    def unpack_second(i, _):
        at = pl.multiple_of(i * 128, 128)
        for block in range(4):
            tiles = g2[block, i].reshape(16, 2, 8, 128)
            even, odd = tiles[:, 0], tiles[:, 1]
            low = jnp.where(rows8 < 4, even, pltpu.roll(odd, 4, 1)).reshape(128, 128)
            high = jnp.where(rows8 < 4, pltpu.roll(even, 4, 1), odd).reshape(128, 128)
            for base, value in ((0, low), (HALF, high)):
                h, l = parts(value)
                lanes = slice(base + block * 128, base + block * 128 + 128)
                b2h[pl.ds(at, 128), lanes] = h
                b2l[pl.ds(at, 128), lanes] = l
        return 0

    lax.fori_loop(0, 4, unpack_second, 0)

    def z_body(i, _):
        at = pl.multiple_of(i * 256, 256)
        value = three(nt, ch[...], cl[...], b2h[pl.ds(at, 256), :], b2l[pl.ds(at, 256), :])
        z_own[:, pl.ds(at, 256)] = value[:ROWS]
        z_out[:, pl.ds(at, 256)] = value[ROWS:]
        return 0

    lax.fori_loop(0, 2, z_body, 0)
    z_wait = place.copy(z_out, z_rx, partner)

    run(gathers1)

    def unpack_first(i, _):
        at = pl.multiple_of(i * 256, 256)
        for block in range(4):
            h, l = parts(g1[block, i].reshape(256, 128))
            b1h[pl.ds(at, 256), block * 128 : block * 128 + 128] = h
            b1l[pl.ds(at, 256), block * 128 : block * 128 + 128] = l
        return 0

    lax.fori_loop(0, 4, unpack_first, 0)
    z_wait()

    def back_body(i, _):
        at = pl.multiple_of(i * 256, 256)
        hot = hot2z[pl.ds(at, 256), :]
        oh, ol = parts(z_own[...])
        rh, rl = parts(z_rx[...])
        value = (nt(oh, hot[:, :HALF]) + nt(ol, hot[:, :HALF])) + (nt(rh, hot[:, HALF:]) + nt(rl, hot[:, HALF:]))
        back[2 * i] = value[:, :128]
        back[2 * i + 1] = value[:, 128:]
        return 0

    lax.fori_loop(0, 4, back_body, 0)
    back_rx[place.chip] = back[place.chip]
    back_waits = []
    for hop, (chip, device) in enumerate(chips):
        source = lax.rem(place.chip + 8 - (hop + 1), 8)
        back_waits.append(place.copy(back.at[chip], back_rx.at[place.chip], device, back_rx.at[source]))

    lane = lax.broadcasted_iota(jnp.int32, (ROWS, 128), 1)

    def mid_body(i, _):
        at = pl.multiple_of(i * 256, 256)
        value = three(nn, p1h[...], p1l[...], b1h[:, pl.ds(at, 256)], b1l[:, pl.ds(at, 256)])
        for k in range(2):
            own = value[:ROWS, k * 128 : k * 128 + 128]
            other = value[ROWS:, k * 128 : k * 128 + 128]
            zero = jnp.where(mine, own, other)
            one = jnp.where(mine, other, own)
            mid[4 * i + 2 * k] = jnp.where(lane < 64, zero, pltpu.roll(one, 64, 1))
            mid[4 * i + 2 * k + 1] = jnp.where(lane < 64, pltpu.roll(zero, 64, 1), one)
        return 0

    lax.fori_loop(0, 2, mid_body, 0)
    mid_rx[place.chip] = mid[place.chip]
    mid_waits = []
    for hop, (chip, device) in enumerate(chips):
        source = lax.rem(place.chip + 8 - (hop + 1), 8)
        mid_waits.append(place.copy(mid.at[chip], mid_rx.at[place.chip], device, mid_rx.at[source]))

    for wait in back_waits:
        wait()
    for pair in range(4):
        even, odd = back_rx[2 * pair], back_rx[2 * pair + 1]
        zero = jnp.where(lane < 64, even, pltpu.roll(odd, 64, 1))
        one = jnp.where(lane < 64, pltpu.roll(even, 64, 1), odd)
        for base, value in ((0, jnp.where(mine, zero, one)), (ROWS, jnp.where(mine, one, zero))):
            h, l = parts(value)
            bmh[base : base + ROWS, pair * 128 : pair * 128 + 128] = h
            bml[base : base + ROWS, pair * 128 : pair * 128 + 128] = l

    def columns(out, lh, ll, rh, rl):
        def body(i, _):
            at = pl.multiple_of(i * 256, 256)
            value = three(tn, lh[:, pl.ds(at, 256)], ll[:, pl.ds(at, 256)], rh(), rl())
            for block in range(4):
                out[block, i] = value[:, block * 128 : block * 128 + 128].reshape(4, 8, 8, 128)
            return 0

        lax.fori_loop(0, 4, body, 0)

    columns(s1, p1h, p1l, lambda: bmh[...], lambda: bml[...])
    scatters1 = [scatter(place, s1, land, *s) for s, land in zip(STREAMS_A, land1)]
    run(scatters1)

    for wait in mid_waits:
        wait()
    for chip in range(8):
        h, l = parts(mid_rx[chip])
        sph[:ROWS, chip * 128 : chip * 128 + 128] = h
        spl[:ROWS, chip * 128 : chip * 128 + 128] = l

    def a2_body(i, _):
        at = pl.multiple_of(i * 256, 256)
        hot = hot2q[:, pl.ds(at, 256)]
        a2_own[:, pl.ds(at, 256)] = nn(sph[:ROWS, :], hot) + nn(spl[:ROWS, :], hot)
        return 0

    lax.fori_loop(0, 4, a2_body, 0)
    a2_wait = place.copy(a2_own, a2_rx, partner)
    run(scatters1)

    def y_body(i, _):
        at = pl.multiple_of(i * 256, 256)
        value = three(nt, bmh[...], bml[...], b1h[pl.ds(at, 256), :], b1l[pl.ds(at, 256), :])
        y_own[:, pl.ds(at, 256)] = value[:ROWS]
        y_out[:, pl.ds(at, 256)] = value[ROWS:]
        return 0

    lax.fori_loop(0, 4, y_body, 0)
    y_wait = place.copy(y_out, y_rx, partner)
    a2_wait()
    split_rows(a2_own, sph, spl, 0)
    split_rows(a2_rx, sph, spl, ROWS)
    side = pl.multiple_of(core * HALF, HALF)
    columns(s2, sph, spl, lambda: ch[:, pl.ds(side, HALF)], lambda: cl[:, pl.ds(side, HALF)])
    scatters2 = [scatter(place, s2, land, *s) for s, land in zip(STREAMS_B, land2)]
    run(scatters2)
    run(scatters1)
    y_wait()

    def sum_rows(i, _):
        at = pl.multiple_of(i * 32, 32)
        h, l = parts(y_own[pl.ds(at, 32), :] + y_rx[pl.ds(at, 32), :])
        p1h[pl.ds(at, 32), :] = h
        p1l[pl.ds(at, 32), :] = l
        return 0

    lax.fori_loop(0, ROWS // 32, sum_rows, 0)

    def grad_stem_body(i, _):
        at = pl.multiple_of(i * 256, 256)
        hot = hot1[pl.ds(at, 256), :]
        grad_stem[:, pl.ds(at, 256)] = nt(p1h[:ROWS, :], hot) + nt(p1l[:ROWS, :], hot)
        return 0

    run(scatters2)
    lax.fori_loop(0, 4, grad_stem_body, 0)
    for _ in range(5):
        run(scatters1)
        run(scatters2)
    run(scatters1)
    factor = 1.0 / (32768.0**0.5)
    grad_first[0] = s1[here].reshape(4, 8, 128) * factor
    first_done = place.copy(grad_first.at[0], grad_first.at[1], partner)
    run(scatters2)
    run(scatters2)
    grad_second[0] = s2[here].reshape(4, 8, 128) * factor
    second_done = place.copy(grad_second.at[0], grad_second.at[1], partner)
    first_done()
    second_done()
    place.close()


def scratch_shapes():
    f32, b16 = (lambda *s: pltpu.VMEM(s, F32)), (lambda *s: pltpu.VMEM(s, BF16))
    shapes = [pltpu.SemaphoreType.DMA((256,)), pltpu.SemaphoreType.DMA((256,))]
    field = (4, 4, 4, 8, 8, 128)
    shapes += [f32(*field), f32(*field), f32(4, 1, 1, 1, 8, 128), f32(ROWS, WIDTH), f32(ROWS, WIDTH)]
    shapes += [b16(WIDTH, WIDTH)] * 3
    shapes += [b16(2 * ROWS, WIDTH)] * 4 + [b16(WIDTH, HALF)] * 2 + [b16(HALF, WIDTH)] * 2
    shapes += [f32(ROWS, HALF)] * 3
    shapes += [f32(8, ROWS, 128)] * 4
    shapes += [b16(2 * ROWS, HALF)] * 2 + [b16(2 * ROWS, WIDTH)] * 2
    shapes += [f32(ROWS, WIDTH)] * 5
    shapes += [f32(*field)] * 2
    for streams in (STREAMS_A, STREAMS_B):
        for _, count, order in streams:
            shapes += [f32(*s) for s in landing_shapes(count, order)]
    return shapes


def on_device(stem_first, cotangent, branch_first, branch_second, bond_first, bond_second):
    core = lax.rem(lax.axis_index("gx"), 2)
    even = core == 0
    rows = branch_first.reshape(4, 4, 2, 2, 64).transpose(3, 1, 0, 2, 4).reshape(2, 4, 4, 128)
    none = jnp.zeros_like(rows)
    first = jnp.concatenate([jnp.where(even, rows, none), jnp.where(even, none, rows)], axis=2)
    first = first.reshape(2, 4, 1, 1, 1, 8, 128)
    second = branch_second.reshape(4, 2, 4, 128).transpose(2, 1, 0, 3).reshape(4, 1, 1, 1, 8, 128)

    def by(bond, axes):
        return bond.reshape(4, 2, 2, 4, 4, 4).transpose(axes).reshape(1, WIDTH)

    bond_q = by(bond_first, (0, 3, 4, 1, 2, 5))
    bond2_q = by(bond_second, (0, 3, 4, 1, 2, 5))
    bond2_z = by(bond_second, (2, 0, 3, 4, 1, 5))
    bond2_z = jnp.where(even, bond2_z, jnp.roll(bond2_z, HALF, axis=1))

    vmem = pl.BlockSpec(memory_space=pltpu.VMEM)
    grad_stem, halves_first, halves_second = pl.pallas_call(
        kernel,
        out_shape=(
            jax.ShapeDtypeStruct((ROWS, WIDTH), F32),
            jax.ShapeDtypeStruct((2, 4, 8, 128), F32),
            jax.ShapeDtypeStruct((2, 4, 8, 128), F32),
        ),
        in_specs=[vmem] * 7,
        out_specs=(vmem,) * 3,
        scratch_shapes=scratch_shapes(),
        compiler_params=pltpu.CompilerParams(
            collective_id=0, has_side_effects=True, vmem_limit_bytes=60 * 2**20
        ),
    )(stem_first.reshape(ROWS, WIDTH), cotangent.reshape(ROWS, WIDTH), first, second, bond_q, bond2_q, bond2_z)

    def own_rows(halves):
        rows = jnp.where(even, halves[:, :, :4], halves[:, :, 4:])
        return jnp.where(even, rows, rows[::-1])

    grad_first = own_rows(halves_first).reshape(2, 4, 4, 2, 64).transpose(2, 1, 3, 0, 4).reshape(4, WIDTH)
    grad_second = own_rows(halves_second).transpose(2, 0, 1, 3).reshape(4, WIDTH)
    return grad_stem.reshape(1, ROWS, WIDTH), grad_first, grad_second


def solution(mesh):
    return jax.shard_map(
        on_device,
        mesh=mesh,
        in_specs=(
            P("gx", "gy", None),
            P("gx", "gy", None),
            P(("gx", "gy"), None),
            P(("gx", "gy"), None),
            P(),
            P(),
        ),
        out_specs=(P("gx", "gy", None), P(("gx", "gy"), None), P(("gx", "gy"), None)),
        check_vma=False,
    )
```

```python
import jax
import jax.numpy as jnp
from jax import lax
from jax.experimental import pallas as pl
from jax.experimental.pallas import tpu as pltpu
from jax.sharding import PartitionSpec as P

MESH = pl.DeviceIdType.MESH
SIZE = {"x": 4, "y": 4, "z": 8}
DIM = {"x": 1, "y": 3, "z": 4}
ROWS = 128
WIDTH = 1024
HALF = 512
F32 = jnp.float32
BF16 = jnp.bfloat16

LINES_A, PLANES_A, LINES_B = (0, 3), (3, 1), (0, 4)
PARTS = ((0, "y", "x"), (1, "x", "y"))


def dot(left, right, over):
    return lax.dot_general(left, right, (over, ((), ())), preferred_element_type=F32)


def nn(left, right):
    return dot(left, right, ((1,), (0,)))


def nt(left, right):
    return dot(left, right, ((1,), (1,)))


def tn(left, right):
    return dot(left, right, ((0,), (0,)))


def three(form, lhi, llo, rhi, rlo):
    return form(lhi, rhi) + (form(lhi, rlo) + form(llo, rhi))


def parts(value):
    high = value.astype(BF16)
    return high, (value - high.astype(F32)).astype(BF16)


class Place:
    def __init__(self, send, recv):
        gx, gy = lax.axis_index("gx"), lax.axis_index("gy")
        self.core = lax.rem(gx, 2)
        self.low = lax.rem(gx // 2, 2)
        self.at = {"x": gx // 4, "y": gy // 4, "z": lax.rem(gy, 4) * 2 + self.low}
        self.chip = gx // 2
        self.send, self.recv = send, recv
        self.used = 0
        self.open = []

    def device(self, core=None, **where):
        spot = {**self.at, **where}
        core = self.core if core is None else core
        gx = (spot["x"] * 2 + lax.rem(spot["z"], 2)) * 2 + core
        return gx, spot["y"] * 4 + spot["z"] // 2

    def step(self, axis, by):
        return lax.rem(self.at[axis] + (by + SIZE[axis]), SIZE[axis])

    def neighbour(self, axis, by):
        return self.device(**{axis: self.step(axis, by)})

    def partner(self):
        return self.device(core=1 - self.core)

    def copy(self, src, dst, device, lands=None):
        slot = self.used
        self.used += 1
        out = pltpu.make_async_remote_copy(
            src_ref=src,
            dst_ref=dst,
            send_sem=self.send.at[slot],
            recv_sem=self.recv.at[slot],
            device_id=device,
            device_id_type=MESH,
        )
        out.start()
        self.open.append(out)
        lands = dst if lands is None else lands
        return pltpu.make_async_remote_copy(
            src_ref=lands,
            dst_ref=lands,
            send_sem=self.send.at[slot],
            recv_sem=self.recv.at[slot],
            device_id=device,
            device_id_type=MESH,
        ).wait_recv

    def close(self):
        for out in self.open:
            out.wait_send()


def view(block, count, spot, cut=None):
    index = [slice(block, block + count)] + [slice(None)] * 6
    for axis, value in spot.items():
        if axis == "z":
            index[2], index[4] = pl.ds(lax.rem(value, 2), 1), pl.ds(value // 2, 1)
        elif axis == "part":
            index[4] = slice(2 * value, 2 * value + 2)
        else:
            index[DIM[axis]] = pl.ds(value, 1)
    if cut is not None:
        name, which = cut
        index[DIM[name]] = slice(which * 2, which * 2 + 2)
    return tuple(index)


def direct(place, axis, own, peer):
    waits = []
    for by in range(1, SIZE[axis]):
        src, dst = own(by)
        waits.append(place.copy(src, dst, place.neighbour(axis, by), peer(by)))
    return waits


def spread(place, buffer, block, count, axis, rest):
    mine = buffer.at[view(block, count, {**rest, axis: place.at[axis]})]
    return direct(
        place,
        axis,
        lambda by: (mine, mine),
        lambda by: buffer.at[view(block, count, {**rest, axis: place.step(axis, -by)})],
    )


def hops():
    return [(dx, dy) for dx in range(4) for dy in range(4) if dx or dy]


def done(waits):
    for wait in waits:
        wait()


def gather_planes(place, buffer, block, count):
    mine = buffer.at[view(block, count, place.at)]
    waits = []
    for dx, dy in hops():
        source = {"x": place.step("x", -dx), "y": place.step("y", -dy), "z": place.at["z"]}
        device = place.device(x=place.step("x", dx), y=place.step("y", dy))
        waits.append(place.copy(mine, mine, device, buffer.at[view(block, count, source)]))
    yield
    done(waits)
    waits = spread(place, buffer, block, count, "z", {})
    yield
    done(waits)
    yield


def gather_lines(place, buffer, block, count):
    waits = spread(place, buffer, block, count, "z", {"x": place.at["x"], "y": place.at["y"]})
    yield
    done(waits)

    def send(part, near, far, line, sign, tick):
        def piece(by):
            spot = {"part": part, near: place.step(near, -line), far: place.step(far, by)}
            return buffer.at[view(block, count, spot)]

        out = piece(-sign * tick)
        return place.copy(out, out, place.neighbour(far, sign), piece(-sign * (tick + 1)))

    ahead, last = [], []

    def ring(part, line, sign):
        ahead.append((part, line, sign, send(*part, line, sign, 0)))
        last.append(send(*part, line, -sign, 0))

    lines = []
    for part, near, far in PARTS:
        lines.append(spread(place, buffer, block, count, near, {"part": part, far: place.at[far]}))
    for part in PARTS:
        ring(part, 0, 1)
    yield
    for line, sign in ((1, -1), (3, 1), (2, -1)):
        for part, waits in zip(PARTS, lines):
            waits[line - 1]()
            ring(part, line, sign)
    yield
    for part, line, sign, wait in ahead:
        wait()
        last.append(send(*part, line, sign, 1))
    yield
    done(last)
    yield


def line_landings(count):
    shapes = [(7, count, 1, 1, 1, 1, 8, 128)]
    for _ in PARTS:
        shapes += [(12, count, 1, 2, 1, 2, 8, 128), (3, count, 1, 2, 1, 2, 8, 128)]
    return shapes


def plane_landings(count):
    return [(7, count, 4, 1, 4, 1, 8, 128), (15, count, 1, 1, 1, 1, 8, 128)]


def collect(buffer, where, waits, landing):
    total = buffer[where]
    for slot, wait in enumerate(waits):
        wait()
        total = total + landing[slot]
    buffer[where] = total


def deliver(place, buffer, block, count, axis, rest, landing):
    return direct(
        place,
        axis,
        lambda by: (buffer.at[view(block, count, {**rest, axis: place.step(axis, by)})], landing.at[by - 1]),
        lambda by: landing.at[by - 1],
    )


def scatter_planes(place, buffer, landings, block, count):
    waits = deliver(place, buffer, block, count, "z", {}, landings[0])
    yield
    collect(buffer, view(block, count, {"z": place.at["z"]}), waits, landings[0])
    waits = []
    for slot, (dx, dy) in enumerate(hops()):
        spot = {"x": place.step("x", dx), "y": place.step("y", dy)}
        src = buffer.at[view(block, count, {**spot, "z": place.at["z"]})]
        waits.append(place.copy(src, landings[1].at[slot], place.device(**spot)))
    yield
    collect(buffer, view(block, count, place.at), waits, landings[1])
    yield


def scatter_lines(place, buffer, landings, block, count):
    last, rings, nears = landings[0], landings[1::2], landings[2::2]

    def send(part, near, far, line, sign, distance, slot):
        def piece(by):
            spot = {"part": part, near: place.step(near, line), far: place.step(far, by)}
            return view(block, count, spot)

        there = rings[part].at[line * 3 + slot]
        wait = place.copy(buffer.at[piece(sign * distance)], there, place.neighbour(far, sign))

        def add():
            wait()
            where = piece(sign * (distance - 1))
            buffer[where] = buffer[where] + there[...]

        return add

    lines = ((2, 1), (1, -1), (0, 1), (3, -1))
    ahead, adds = [], {}
    for line, sign in lines:
        for part in PARTS:
            ahead.append((part, line, sign, send(*part, line, sign, 2, 0)))
    for line, sign in lines:
        for part in PARTS:
            adds[part, line] = [send(*part, line, -sign, 1, 2)]
    yield
    for part, line, sign, add in ahead:
        add()
        adds[part, line].append(send(*part, line, sign, 1, 1))
    yield
    waits = [[None] * 3 for _ in PARTS]
    for line in (2, 1, 3, 0):
        for part in PARTS:
            done(adds[part, line])
            which, near, far = part
            if line:
                src = buffer.at[view(block, count, {"part": which, near: place.step(near, line), far: place.at[far]})]
                waits[which][line - 1] = place.copy(src, nears[which].at[line - 1], place.neighbour(near, line))
    yield
    spot = {"x": place.at["x"], "y": place.at["y"]}
    for part, _, _ in PARTS:
        collect(buffer, view(block, count, {**spot, "part": part}), waits[part], nears[part])
    waits = deliver(place, buffer, block, count, "z", spot, last)
    yield
    collect(buffer, view(block, count, place.at), waits, last)
    yield


def run(*streams):
    for stream in streams:
        next(stream)


def kernel(
    stem_hbm, cotan_hbm, branch_first, branch_second, bond_first, bond_second,
    grad_stem, grad_first, grad_second,
    *scratch,
):
    scratch = list(scratch)

    def take(n=None):
        if n is None:
            return scratch.pop(0)
        return [scratch.pop(0) for _ in range(n)]

    send, recv, local = take(3)
    stem_in, cotan_in, bq1, bq2, bz2, first_in, ends = take(7)
    g1, g2, rx1, stem_rx, cotan_rx = take(5)
    hot1, hot2q, hot2z = take(3)
    p1h, p1l, ch, cl, b1h, b1l, b2h, b2l = take(8)
    z_own, z_out, z_rx = take(3)
    back, back_rx, mid, mid_rx = take(4)
    bmh, bml, sph, spl = take(4)
    y_own, y_out, y_rx, a2_own, a2_rx = take(5)
    a2h, a2l = take(2)
    s1, s2 = take(2)
    land1, land1w, land2 = take(5), take(2), take(5)

    place = Place(send, recv)
    core = place.core
    mine = core == 0

    barrier = pltpu.get_barrier_semaphore()
    chips = []
    for hop in range(1, 8):
        chip = lax.rem(place.chip + hop, 8)
        chips.append((chip, (chip * 2 + core, lax.axis_index("gy"))))
    peers = [place.partner()]
    for axis in "xyz":
        peers += [place.neighbour(axis, by) for by in range(1, SIZE[axis])]
    beside = place.at["z"] + 1 - 2 * place.low
    peers += [place.device(x=place.step("x", by), z=beside) for by in range(1, 4)]
    peers += [place.device(x=place.step("x", dx), y=place.step("y", dy)) for dx, dy in hops() if dx and dy]
    for peer in peers:
        pl.semaphore_signal(barrier, inc=1, device_id=peer, device_id_type=MESH)

    stem_load = pltpu.make_async_copy(stem_hbm, stem_in, local.at[0])
    stem_load.start()
    cotan_load = pltpu.make_async_copy(cotan_hbm, cotan_in, local.at[1])
    cotan_load.start()

    here = view(0, 4, place.at)
    lane4 = lax.broadcasted_iota(jnp.int32, (4, 128), 1)

    def halves(even, odd, lanes):
        return jnp.where(lanes < 64, even, pltpu.roll(odd, 64, 1)), jnp.where(lanes < 64, pltpu.roll(even, 64, 1), odd)

    for block in range(4):
        lanes = slice(block * 128, block * 128 + 128)
        tile = jnp.concatenate([branch_second[:, lanes], branch_second[:, HALF + block * 128 : HALF + block * 128 + 128]], 0)
        g2[view(block, 1, place.at)] = tile.reshape(1, 1, 1, 1, 1, 8, 128)
        pair = halves(
            branch_first[:, block * 256 : block * 256 + 128], branch_first[:, block * 256 + 128 : block * 256 + 256], lane4
        )
        for side in range(2):
            none = jnp.zeros_like(pair[side])
            tile = jnp.where(mine, jnp.concatenate([pair[side], none], 0), jnp.concatenate([none, pair[side]], 0))
            first_in[side, block] = tile.reshape(1, 1, 1, 1, 8, 128)

    def digit(row, lanes):
        return jnp.where(row == lax.rem(lanes // 4, 2) * 64 + lanes // 8 * 4 + lax.rem(lanes, 4), 1.0, 0.0).astype(BF16)

    shuffle = digit(lax.broadcasted_iota(jnp.int32, (128, 128), 0), lax.broadcasted_iota(jnp.int32, (128, 128), 1))
    for bond, out in ((bond_first, bq1), (bond_second, bq2)):
        value = bond[...]
        high = (value // 32).astype(F32).astype(BF16)
        low = lax.rem(value, 32).astype(F32).astype(BF16)
        out[...] = nn(high, shuffle) * 32.0 + nn(low, shuffle)
    lane1 = lax.broadcasted_iota(jnp.int32, (1, 128), 1)
    for pair in range(4):
        zero, one = halves(bond_second[2 * pair : 2 * pair + 1, :], bond_second[2 * pair + 1 : 2 * pair + 2, :], lane1)
        bz2[pair : pair + 1, :] = jnp.where(mine, zero, one).astype(F32)
        bz2[pair + 4 : pair + 5, :] = jnp.where(mine, one, zero).astype(F32)

    pl.semaphore_wait(barrier, len(peers))

    partner = place.partner()
    first_wait = place.copy(first_in.at[1 - core], rx1, partner)
    lines1 = gather_lines(place, g1, *LINES_B)
    lines2, planes2 = gather_lines(place, g2, *LINES_A), gather_planes(place, g2, *PLANES_A)
    run(planes2)
    first_wait()
    g1[here] = first_in[core] + rx1[...]
    run(lines1)
    stem_load.wait()
    cotan_load.wait()
    stem_wait = place.copy(stem_in, stem_rx, partner)
    cotan_wait = place.copy(cotan_in, cotan_rx, partner)

    def build(hot, bond):
        def body(i, _):
            at = pl.multiple_of(i * 64, 64)
            rows = (lax.broadcasted_iota(jnp.int32, (64, 128), 0) + at).astype(F32)
            for group in range(8):
                hit = rows == bond[group : group + 1, :]
                hot[pl.ds(at, 64), group * 128 : group * 128 + 128] = jnp.where(hit, 1.0, 0.0).astype(BF16)
            return 0

        lax.fori_loop(0, WIDTH // 64, body, 0)

    def split_rows(src, high, low, base):
        def body(i, _):
            at = pl.multiple_of(i * 32, 32)
            h, l = parts(src[pl.ds(at, 32), :])
            high[pl.ds(base + at, 32), :] = h
            low[pl.ds(base + at, 32), :] = l
            return 0

        lax.fori_loop(0, src.shape[0] // 32, body, 0)

    build(hot1, bq1)
    split_rows(stem_in, sph, spl, 0)
    stem_wait()
    split_rows(stem_rx, sph, spl, ROWS)

    def permute_stem(i, _):
        at = pl.multiple_of(i * 256, 256)
        hot = hot1[:, pl.ds(at, 256)]
        p1h[:, pl.ds(at, 256)] = nn(sph[...], hot).astype(BF16)
        p1l[:, pl.ds(at, 256)] = nn(spl[...], hot).astype(BF16)
        return 0

    lax.fori_loop(0, 4, permute_stem, 0)
    split_rows(cotan_in, ch, cl, 0)
    cotan_wait()
    split_rows(cotan_rx, ch, cl, ROWS)
    run(lines1, lines2, planes2)
    build(hot2q, bq2)
    run(lines1, lines2)
    build(hot2z, bz2)
    run(lines1, lines2)

    lane = lax.broadcasted_iota(jnp.int32, (ROWS, 128), 1)

    run(lines1)

    def unpack_first(i, _):
        at = pl.multiple_of(i * 256, 256)
        for block in range(4):
            h, l = parts(g1[block, i].reshape(256, 128))
            b1h[pl.ds(at, 256), block * 128 : block * 128 + 128] = h
            b1l[pl.ds(at, 256), block * 128 : block * 128 + 128] = l
        return 0

    lax.fori_loop(0, 4, unpack_first, 0)

    def mid_body(i, _):
        at = pl.multiple_of(i * 256, 256)
        value = three(nn, p1h[...], p1l[...], b1h[:, pl.ds(at, 256)], b1l[:, pl.ds(at, 256)])
        for k in range(2):
            own = value[:ROWS, k * 128 : k * 128 + 128]
            other = value[ROWS:, k * 128 : k * 128 + 128]
            zero = jnp.where(mine, own, other)
            one = jnp.where(mine, other, own)
            mid[4 * i + 2 * k] = jnp.where(lane < 64, zero, pltpu.roll(one, 64, 1))
            mid[4 * i + 2 * k + 1] = jnp.where(lane < 64, pltpu.roll(zero, 64, 1), one)
        return 0

    lax.fori_loop(0, 2, mid_body, 0)
    run(lines2)
    mid_rx[place.chip] = mid[place.chip]
    mid_waits = []
    for hop, (chip, device) in enumerate(chips):
        source = lax.rem(place.chip + 8 - (hop + 1), 8)
        mid_waits.append(place.copy(mid.at[chip], mid_rx.at[place.chip], device, mid_rx.at[source]))

    run(lines2, planes2)
    rows8 = lax.broadcasted_iota(jnp.int32, (16, 8, 128), 1)

    def unpack_second(i, _):
        at = pl.multiple_of(i * 128, 128)
        for block in range(4):
            tiles = g2[block, i].reshape(16, 2, 8, 128)
            even, odd = tiles[:, 0], tiles[:, 1]
            low = jnp.where(rows8 < 4, even, pltpu.roll(odd, 4, 1)).reshape(128, 128)
            high = jnp.where(rows8 < 4, pltpu.roll(even, 4, 1), odd).reshape(128, 128)
            for base, value in ((0, low), (HALF, high)):
                h, l = parts(value)
                lanes = slice(base + block * 128, base + block * 128 + 128)
                b2h[pl.ds(at, 128), lanes] = h
                b2l[pl.ds(at, 128), lanes] = l
        return 0

    lax.fori_loop(0, 4, unpack_second, 0)

    def z_body(i, _):
        at = pl.multiple_of(i * 256, 256)
        value = three(nt, ch[...], cl[...], b2h[pl.ds(at, 256), :], b2l[pl.ds(at, 256), :])
        z_own[:, pl.ds(at, 256)] = value[:ROWS]
        z_out[:, pl.ds(at, 256)] = value[ROWS:]
        return 0

    z_waits = []
    for i in range(2):
        z_body(i, 0)
        block = (slice(None), slice(i * 256, i * 256 + 256))
        z_waits.append(place.copy(z_out.at[block], z_rx.at[block], partner))
    def column_block(out, i, lh, ll, rh, rl):
        value = three(tn, lh, ll, rh, rl)
        for block in range(4):
            out[block, i] = value[:, block * 128 : block * 128 + 128].reshape(2, 4, 4, 8, 128)

    done(mid_waits)
    for chip in range(8):
        h, l = parts(mid_rx[chip])
        sph[:ROWS, chip * 128 : chip * 128 + 128] = h
        spl[:ROWS, chip * 128 : chip * 128 + 128] = l

    side = pl.multiple_of(core * HALF, HALF)
    a2_waits = []
    for i in range(4):
        lanes = slice(i * 256, i * 256 + 256)
        value = nn(sph[:ROWS, :], hot2q[:, lanes]) + nn(spl[:ROWS, :], hot2q[:, lanes])
        a2_own[:, lanes] = value
        a2_waits.append(place.copy(a2_own.at[:, lanes], a2_rx.at[:, lanes], partner))
        a2h[:ROWS, lanes], a2l[:ROWS, lanes] = parts(value)
    done(z_waits)
    split_rows(z_own, bmh, bml, 0)
    split_rows(z_rx, bmh, bml, ROWS)

    bit, pair = lax.rem(place.chip, 2), place.chip // 2
    back_waits = []
    for turn in (1, 2, 3, 0):
        to, source = lax.rem(pair + turn, 4), lax.rem(pair + 4 - turn, 4)
        hot = hot2z[pl.ds(pl.multiple_of(to * 256, 256), 256), :]
        value = nt(bmh[:ROWS], hot[:, :HALF]) + nt(bml[:ROWS], hot[:, :HALF])
        value = value + (nt(bmh[ROWS:], hot[:, HALF:]) + nt(bml[ROWS:], hot[:, HALF:]))
        back[2 * to] = value[:, :128]
        back[2 * to + 1] = value[:, 128:]
        for half in (bit, 1 - bit) if turn else (1 - bit,):
            chip = to * 2 + half
            device = chip * 2 + core, lax.axis_index("gy")
            back_waits.append(place.copy(back.at[chip], back_rx.at[place.chip], device, back_rx.at[source * 2 + half]))
    back_rx[place.chip] = back[place.chip]

    for i in range(4):
        lanes = slice(i * 256, i * 256 + 256)
        done(a2_waits[i : i + 1])
        a2h[ROWS:, lanes], a2l[ROWS:, lanes] = parts(a2_rx[:, lanes])
        column_block(s2, i, a2h[:, lanes], a2l[:, lanes], ch[:, pl.ds(side, HALF)], cl[:, pl.ds(side, HALF)])
    back2 = scatter_lines(place, s2, land2, *LINES_B)
    run(back2)

    done(back_waits)
    for pair in range(4):
        even, odd = back_rx[2 * pair], back_rx[2 * pair + 1]
        zero = jnp.where(lane < 64, even, pltpu.roll(odd, 64, 1))
        one = jnp.where(lane < 64, pltpu.roll(even, 64, 1), odd)
        for base, value in ((0, jnp.where(mine, zero, one)), (ROWS, jnp.where(mine, one, zero))):
            h, l = parts(value)
            bmh[base : base + ROWS, pair * 128 : pair * 128 + 128] = h
            bml[base : base + ROWS, pair * 128 : pair * 128 + 128] = l

    def first_body(i, _):
        at = pl.multiple_of(i * 256, 256)
        column_block(s1, i, p1h[:, pl.ds(at, 256)], p1l[:, pl.ds(at, 256)], bmh[...], bml[...])
        return 0

    lax.fori_loop(0, 4, first_body, 0)
    back1, back1w = scatter_lines(place, s1, land1, *LINES_A), scatter_planes(place, s1, land1w, *PLANES_A)
    run(back1, back1w, back2, back1, back2)

    def y_body(i, _):
        at = pl.multiple_of(i * 256, 256)
        value = three(nt, bmh[...], bml[...], b1h[pl.ds(at, 256), :], b1l[pl.ds(at, 256), :])
        y_own[:, pl.ds(at, 256)] = value[:ROWS]
        y_out[:, pl.ds(at, 256)] = value[ROWS:]
        return 0

    lax.fori_loop(0, 4, y_body, 0)
    y_wait = place.copy(y_out, y_rx, partner)
    run(back1, back2, back1w)
    y_wait()

    def sum_rows(i, _):
        at = pl.multiple_of(i * 32, 32)
        h, l = parts(y_own[pl.ds(at, 32), :] + y_rx[pl.ds(at, 32), :])
        p1h[pl.ds(at, 32), :] = h
        p1l[pl.ds(at, 32), :] = l
        return 0

    lax.fori_loop(0, ROWS // 32, sum_rows, 0)

    def grad_stem_body(i, _):
        at = pl.multiple_of(i * 256, 256)
        hot = hot1[pl.ds(at, 256), :]
        grad_stem[:, pl.ds(at, 256)] = nt(p1h[:ROWS, :], hot) + nt(p1l[:ROWS, :], hot)
        return 0

    lax.fori_loop(0, 4, grad_stem_body, 0)
    run(back1, back2)
    factor = 1.0 / (32768.0**0.5)
    ends[2] = s2[here].reshape(4, 8, 128) * factor
    second_done = place.copy(ends.at[2], ends.at[3], partner)

    def own_rows(tile):
        return jnp.where(mine, tile[:4], tile[4:])

    second_done()
    for block in range(4):
        own, other = own_rows(ends[2, block]), own_rows(ends[3, block])
        grad_second[:, block * 128 : block * 128 + 128] = jnp.where(mine, own, other)
        grad_second[:, HALF + block * 128 : HALF + block * 128 + 128] = jnp.where(mine, other, own)
    run(back1, back1w)
    ends[0] = s1[here].reshape(4, 8, 128) * factor
    first_done = place.copy(ends.at[0], ends.at[1], partner)
    first_done()
    for block in range(4):
        own, other = own_rows(ends[0, block]), own_rows(ends[1, block])
        left, right = halves(jnp.where(mine, own, other), jnp.where(mine, other, own), lane4)
        grad_first[:, block * 256 : block * 256 + 128] = left
        grad_first[:, block * 256 + 128 : block * 256 + 256] = right
    place.close()


def scratch_shapes():
    f32, b16 = (lambda *s: pltpu.VMEM(s, F32)), (lambda *s: pltpu.VMEM(s, BF16))
    shapes = [pltpu.SemaphoreType.DMA((256,)), pltpu.SemaphoreType.DMA((256,)), pltpu.SemaphoreType.DMA((2,))]
    field = (4, 4, 2, 4, 4, 8, 128)
    shapes += [f32(ROWS, WIDTH), f32(ROWS, WIDTH), f32(8, 128), f32(8, 128), f32(8, 128)]
    shapes += [f32(2, 4, 1, 1, 1, 1, 8, 128), f32(4, 4, 8, 128)]
    shapes += [f32(*field), f32(*field), f32(4, 1, 1, 1, 1, 8, 128), f32(ROWS, WIDTH), f32(ROWS, WIDTH)]
    shapes += [b16(WIDTH, WIDTH)] * 3
    shapes += [b16(2 * ROWS, WIDTH)] * 4 + [b16(WIDTH, HALF)] * 2 + [b16(HALF, WIDTH)] * 2
    shapes += [f32(ROWS, HALF)] * 3
    shapes += [f32(8, ROWS, 128)] * 4
    shapes += [b16(2 * ROWS, HALF)] * 2 + [b16(2 * ROWS, WIDTH)] * 2
    shapes += [f32(ROWS, WIDTH)] * 5 + [b16(2 * ROWS, WIDTH)] * 2
    shapes += [f32(*field)] * 2
    for dims in (line_landings(LINES_A[1]), plane_landings(PLANES_A[1]), line_landings(LINES_B[1])):
        shapes += [f32(*dim) for dim in dims]
    return shapes


def on_device(stem_first, cotangent, branch_first, branch_second, bond_first, bond_second):
    vmem, anywhere = pl.BlockSpec(memory_space=pltpu.VMEM), pl.BlockSpec(memory_space=pl.ANY)
    grad_stem, grad_first, grad_second = pl.pallas_call(
        kernel,
        out_shape=(
            jax.ShapeDtypeStruct((ROWS, WIDTH), F32),
            jax.ShapeDtypeStruct((4, WIDTH), F32),
            jax.ShapeDtypeStruct((4, WIDTH), F32),
        ),
        in_specs=[anywhere, anywhere] + [vmem] * 4,
        out_specs=(vmem,) * 3,
        scratch_shapes=scratch_shapes(),
        compiler_params=pltpu.CompilerParams(
            collective_id=0, has_side_effects=True, vmem_limit_bytes=60 * 2**20
        ),
    )(
        stem_first.reshape(ROWS, WIDTH),
        cotangent.reshape(ROWS, WIDTH),
        branch_first,
        branch_second,
        bond_first.reshape(8, 128),
        bond_second.reshape(8, 128),
    )
    return grad_stem.reshape(1, ROWS, WIDTH), grad_first, grad_second


def solution(mesh):
    return jax.shard_map(
        on_device,
        mesh=mesh,
        in_specs=(
            P("gx", "gy", None),
            P("gx", "gy", None),
            P(("gx", "gy"), None),
            P(("gx", "gy"), None),
            P(),
            P(),
        ),
        out_specs=(P("gx", "gy", None), P(("gx", "gy"), None), P(("gx", "gy"), None)),
        check_vma=False,
    )
```

```python
import jax
import jax.numpy as jnp
from jax import lax
from jax.experimental import pallas as pl
from jax.experimental.pallas import tpu as pltpu
from jax.sharding import PartitionSpec as P

MESH = pl.DeviceIdType.MESH
SIZE = {"x": 4, "y": 4, "z": 8}
DIM = {"x": 1, "y": 3, "z": 4}
ROWS = 128
WIDTH = 1024
HALF = 512
F32 = jnp.float32
BF16 = jnp.bfloat16

LINES_A, PLANES_A, LINES_B = (0, 3), (3, 1), (0, 4)
GROUPS = 56
PARTS = ((0, "y", "x"), (1, "x", "y"))


def dot(left, right, over):
    return lax.dot_general(left, right, (over, ((), ())), preferred_element_type=F32)


def nn(left, right):
    return dot(left, right, ((1,), (0,)))


def nt(left, right):
    return dot(left, right, ((1,), (1,)))


def tn(left, right):
    return dot(left, right, ((0,), (0,)))


def three(form, lhi, llo, rhi, rlo):
    return form(lhi, rhi) + (form(lhi, rlo) + form(llo, rhi))


def parts(value):
    high = value.astype(BF16)
    return high, (value - high.astype(F32)).astype(BF16)


class Place:
    def __init__(self, send, recv):
        gx, gy = lax.axis_index("gx"), lax.axis_index("gy")
        self.core = lax.rem(gx, 2)
        self.low = lax.rem(gx // 2, 2)
        self.at = {"x": gx // 4, "y": gy // 4, "z": lax.rem(gy, 4) * 2 + self.low}
        self.chip = gx // 2
        self.send, self.recv = send, recv
        self.used = 0
        self.drained = 0
        self.open = []

    def device(self, core=None, **where):
        spot = {**self.at, **where}
        core = self.core if core is None else core
        gx = (spot["x"] * 2 + lax.rem(spot["z"], 2)) * 2 + core
        return gx, spot["y"] * 4 + spot["z"] // 2

    def step(self, axis, by):
        return lax.rem(self.at[axis] + (by + SIZE[axis]), SIZE[axis])

    def neighbour(self, axis, by):
        return self.device(**{axis: self.step(axis, by)})

    def partner(self):
        return self.device(core=1 - self.core)

    def transfer(self, src, dst, slot, device):
        return pltpu.make_async_remote_copy(
            src_ref=src,
            dst_ref=dst,
            send_sem=self.send.at[slot],
            recv_sem=self.recv.at[slot],
            device_id=device,
            device_id_type=MESH,
        )

    def group(self, whole):
        slot = self.used
        self.used += 1
        together = self.transfer(whole, whole, slot, self.partner())
        self.open.append(together)

        def copy(src, dst, device):
            self.transfer(src, dst, slot, device).start()

        return copy, together.wait_recv

    def copy(self, src, dst, device):
        copy, wait = self.group(dst)
        copy(src, dst, device)
        return wait

    def sent(self, count=None):
        count = self.used if count is None else count
        for out in self.open[self.drained : count]:
            out.wait_send()
        self.drained = max(self.drained, count)


def view(block, count, spot, cut=None):
    index = [slice(block, block + count)] + [slice(None)] * 6
    for axis, value in spot.items():
        if axis == "z":
            index[2], index[4] = pl.ds(lax.rem(value, 2), 1), pl.ds(value // 2, 1)
        elif axis == "part":
            index[4] = slice(2 * value, 2 * value + 2)
        else:
            index[DIM[axis]] = pl.ds(value, 1)
    if cut is not None:
        name, which = cut
        index[DIM[name]] = slice(which * 2, which * 2 + 2)
    return tuple(index)


def hops():
    return [(dx, dy) for dx in range(4) for dy in range(4) if dx or dy]


def done(waits):
    for wait in waits:
        wait()


def spread(place, buffer, block, count, axis, rest, whole):
    mine = buffer.at[view(block, count, {**rest, axis: place.at[axis]})]
    copy, wait = place.group(whole)
    for by in range(1, SIZE[axis]):
        copy(mine, mine, place.neighbour(axis, by))
    return wait


def gather_planes(place, buffer, sizes, block, count):
    mine = buffer.at[view(block, count, place.at)]
    copy, wait = place.group(sizes[1])
    for dx, dy in hops():
        copy(mine, mine, place.device(x=place.step("x", dx), y=place.step("y", dy)))
    yield
    wait()
    wait = spread(place, buffer, block, count, "z", {}, sizes[0])
    yield
    wait()
    yield


def gather_lines(place, buffer, sizes, block, count):
    wait = spread(place, buffer, block, count, "z", {"x": place.at["x"], "y": place.at["y"]}, sizes[0])
    yield
    wait()
    both = buffer.at[block : block + count, 0:1, :, 0:1]
    near_groups = [place.group(both) for _ in range(3)]
    ahead = {line: place.group(both) for line in range(4)}
    last, last_wait = place.group(buffer.at[block : block + count, 0:2])

    def send(copy, part, near, far, line, sign, tick):
        spot = {"part": part, near: place.step(near, -line), far: place.step(far, -sign * tick)}
        out = buffer.at[view(block, count, spot)]
        copy(out, out, place.neighbour(far, sign))

    def ring(line, sign):
        for part in PARTS:
            send(ahead[line][0], *part, line, sign, 0)
            send(last, *part, line, -sign, 0)

    for part, near, far in PARTS:
        mine = buffer.at[view(block, count, {"part": part, near: place.at[near], far: place.at[far]})]
        for by in range(1, 4):
            near_groups[by - 1][0](mine, mine, place.neighbour(near, by))
    ring(0, 1)
    yield
    order = ((1, -1), (3, 1), (2, -1))
    for line, sign in order:
        near_groups[line - 1][1]()
        ring(line, sign)
    yield
    for line, sign in ((0, 1), *order):
        ahead[line][1]()
        for part in PARTS:
            send(last, *part, line, sign, 1)
    yield
    last_wait()
    yield


def line_landings(count):
    shapes = [(7, count, 1, 1, 1, 1, 8, 128)]
    for _ in PARTS:
        shapes += [(12, count, 1, 2, 1, 2, 8, 128), (3, count, 1, 2, 1, 2, 8, 128)]
    return shapes


def plane_landings(count):
    return [(7, count, 4, 1, 4, 1, 8, 128), (15, count, 1, 1, 1, 1, 8, 128)]


def collect(buffer, where, landing):
    total = buffer[where]
    for slot in range(landing.shape[0]):
        total = total + landing[slot]
    buffer[where] = total


def deliver(place, buffer, block, count, axis, rest, landing):
    copy, wait = place.group(landing)
    for by in range(1, SIZE[axis]):
        src = buffer.at[view(block, count, {**rest, axis: place.step(axis, by)})]
        copy(src, landing.at[by - 1], place.neighbour(axis, by))
    return wait


def scatter_planes(place, buffer, landings, block, count):
    wait = deliver(place, buffer, block, count, "z", {}, landings[0])
    yield
    wait()
    collect(buffer, view(block, count, {"z": place.at["z"]}), landings[0])
    copy, wait = place.group(landings[1])
    for slot, (dx, dy) in enumerate(hops()):
        spot = {"x": place.step("x", dx), "y": place.step("y", dy)}
        src = buffer.at[view(block, count, {**spot, "z": place.at["z"]})]
        copy(src, landings[1].at[slot], place.device(**spot))
    yield
    wait()
    collect(buffer, view(block, count, place.at), landings[1])
    yield


def scatter_lines(place, buffer, landings, block, count):
    last, rings, nears = landings[0], landings[1::2], landings[2::2]
    lines = ((2, 1), (1, -1), (0, 1), (3, -1))
    ahead = {line: place.group(rings[0].at[0:2]) for line in range(4)}
    close = {line: place.group(rings[0].at[0:4]) for line in range(4)}

    def piece(part, near, far, line, by):
        return view(block, count, {"part": part, near: place.step(near, line), far: place.step(far, by)})

    def send(copy, part, near, far, line, sign, distance, slot):
        there = rings[part].at[line * 3 + slot]
        copy(buffer.at[piece(part, near, far, line, sign * distance)], there, place.neighbour(far, sign))

    for line, sign in lines:
        for part in PARTS:
            send(ahead[line][0], *part, line, sign, 2, 0)
    for line, sign in lines:
        for part in PARTS:
            send(close[line][0], *part, line, -sign, 1, 2)
    yield
    for line, sign in lines:
        ahead[line][1]()
        for part in PARTS:
            where = piece(*part, line, sign)
            buffer[where] = buffer[where] + rings[part[0]][line * 3]
            send(close[line][0], *part, line, sign, 1, 1)
    yield
    copy, wait = place.group(rings[0].at[0:6])
    for line in (2, 1, 3, 0):
        close[line][1]()
        for part in PARTS:
            where = piece(*part, line, 0)
            which, near, far = part
            buffer[where] = buffer[where] + (rings[which][line * 3 + 1] + rings[which][line * 3 + 2])
            if line:
                copy(buffer.at[where], nears[which].at[line - 1], place.neighbour(near, line))
    yield
    wait()
    spot = {"x": place.at["x"], "y": place.at["y"]}
    for part, _, _ in PARTS:
        collect(buffer, view(block, count, {**spot, "part": part}), nears[part])
    wait = deliver(place, buffer, block, count, "z", spot, last)
    yield
    wait()
    collect(buffer, view(block, count, place.at), last)
    yield


def run(*streams):
    for stream in streams:
        next(stream)


def kernel(
    stem_hbm, cotan_hbm, branch_first, branch_second, bond_first, bond_second,
    grad_stem, grad_first, grad_second,
    *scratch,
):
    scratch = list(scratch)

    def take(n=None):
        if n is None:
            return scratch.pop(0)
        return [scratch.pop(0) for _ in range(n)]

    send, recv, local = take(3)
    stem_in, cotan_in, bq1, bq2, bz2, first_in, ends = take(7)
    g1, g2, rx1, stem_rx, cotan_rx = take(5)
    hot1, hot2q, hot2z = take(3)
    p1h, p1l, ch, cl, b1h, b1l, b2h, b2l = take(8)
    z_own, z_out, z_rx = take(3)
    back, back_rx, mid, mid_rx = take(4)
    bmh, bml, sph, spl = take(4)
    y_own, y_out, y_rx, a2_own, a2_rx = take(5)
    a2h, a2l = take(2)
    s1, s2 = take(2)
    land1, land1w, land2 = take(5), take(2), take(5)

    place = Place(send, recv)
    core = place.core
    mine = core == 0

    barrier = pltpu.get_barrier_semaphore()
    chips = []
    for hop in range(1, 8):
        chip = lax.rem(place.chip + hop, 8)
        chips.append((chip, (chip * 2 + core, lax.axis_index("gy"))))
    peers = [place.partner()]
    for axis in "xyz":
        peers += [place.neighbour(axis, by) for by in range(1, SIZE[axis])]
    beside = place.at["z"] + 1 - 2 * place.low
    peers += [place.device(x=place.step("x", by), z=beside) for by in range(1, 4)]
    peers += [place.device(x=place.step("x", dx), y=place.step("y", dy)) for dx, dy in hops() if dx and dy]
    for peer in peers:
        pl.semaphore_signal(barrier, inc=1, device_id=peer, device_id_type=MESH)

    stem_load = pltpu.make_async_copy(stem_hbm, stem_in, local.at[0])
    stem_load.start()
    cotan_load = pltpu.make_async_copy(cotan_hbm, cotan_in, local.at[1])
    cotan_load.start()

    here = view(0, 4, place.at)
    lane4 = lax.broadcasted_iota(jnp.int32, (4, 128), 1)

    def folded(value):
        return value[:ROWS] + value[ROWS:]

    def halves(even, odd, lanes):
        return jnp.where(lanes < 64, even, pltpu.roll(odd, 64, 1)), jnp.where(lanes < 64, pltpu.roll(even, 64, 1), odd)

    for block in range(4):
        lanes = slice(block * 128, block * 128 + 128)
        tile = jnp.concatenate([branch_second[:, lanes], branch_second[:, HALF + block * 128 : HALF + block * 128 + 128]], 0)
        g2[view(block, 1, place.at)] = tile.reshape(1, 1, 1, 1, 1, 8, 128)
        pair = halves(
            branch_first[:, block * 256 : block * 256 + 128], branch_first[:, block * 256 + 128 : block * 256 + 256], lane4
        )
        for side in range(2):
            none = jnp.zeros_like(pair[side])
            tile = jnp.where(mine, jnp.concatenate([pair[side], none], 0), jnp.concatenate([none, pair[side]], 0))
            first_in[side, block] = tile.reshape(1, 1, 1, 1, 8, 128)

    def digit(row, lanes):
        return jnp.where(row == lax.rem(lanes // 4, 2) * 64 + lanes // 8 * 4 + lax.rem(lanes, 4), 1.0, 0.0).astype(BF16)

    shuffle = digit(lax.broadcasted_iota(jnp.int32, (128, 128), 0), lax.broadcasted_iota(jnp.int32, (128, 128), 1))
    for bond, out in ((bond_first, bq1), (bond_second, bq2)):
        value = bond[...]
        high = (value // 32).astype(F32).astype(BF16)
        low = lax.rem(value, 32).astype(F32).astype(BF16)
        out[...] = nn(high, shuffle) * 32.0 + nn(low, shuffle)
    lane1 = lax.broadcasted_iota(jnp.int32, (1, 128), 1)
    for pair in range(4):
        zero, one = halves(bond_second[2 * pair : 2 * pair + 1, :], bond_second[2 * pair + 1 : 2 * pair + 2, :], lane1)
        bz2[pair : pair + 1, :] = jnp.where(mine, zero, one).astype(F32)
        bz2[pair + 4 : pair + 5, :] = jnp.where(mine, one, zero).astype(F32)

    pl.semaphore_wait(barrier, len(peers))

    partner = place.partner()
    first_wait = place.copy(first_in.at[1 - core], rx1, partner)
    lines1 = gather_lines(place, g1, land2, *LINES_B)
    lines2, planes2 = gather_lines(place, g2, land1, *LINES_A), gather_planes(place, g2, land1w, *PLANES_A)
    run(planes2)
    first_wait()
    g1[here] = first_in[core] + rx1[...]
    run(lines1)
    stem_load.wait()
    cotan_load.wait()
    stem_wait = place.copy(stem_in, stem_rx, partner)
    cotan_wait = place.copy(cotan_in, cotan_rx, partner)

    def build(hot, bond):
        def body(i, _):
            at = pl.multiple_of(i * 64, 64)
            rows = (lax.broadcasted_iota(jnp.int32, (64, 128), 0) + at).astype(F32)
            for group in range(8):
                hit = rows == bond[group : group + 1, :]
                hot[pl.ds(at, 64), group * 128 : group * 128 + 128] = jnp.where(hit, 1.0, 0.0).astype(BF16)
            return 0

        lax.fori_loop(0, WIDTH // 64, body, 0)

    def split_rows(src, high, low, base):
        def body(i, _):
            at = pl.multiple_of(i * 32, 32)
            h, l = parts(src[pl.ds(at, 32), :])
            high[pl.ds(base + at, 32), :] = h
            low[pl.ds(base + at, 32), :] = l
            return 0

        lax.fori_loop(0, src.shape[0] // 32, body, 0)

    build(hot1, bq1)
    split_rows(stem_in, sph, spl, 0)
    stem_wait()
    split_rows(stem_rx, sph, spl, ROWS)

    def permute_stem(i, _):
        at = pl.multiple_of(i * 256, 256)
        hot = hot1[:, pl.ds(at, 256)]
        p1h[:, pl.ds(at, 256)] = nn(sph[...], hot).astype(BF16)
        p1l[:, pl.ds(at, 256)] = nn(spl[...], hot).astype(BF16)
        return 0

    lax.fori_loop(0, 4, permute_stem, 0)
    split_rows(cotan_in, ch, cl, 0)
    cotan_wait()
    split_rows(cotan_rx, ch, cl, ROWS)
    run(lines1, lines2, planes2)
    build(hot2q, bq2)
    run(lines1, lines2)
    build(hot2z, bz2)
    run(lines1, lines2)

    lane = lax.broadcasted_iota(jnp.int32, (ROWS, 128), 1)

    run(lines1)

    def unpack_first(i, _):
        at = pl.multiple_of(i * 256, 256)
        for block in range(4):
            h, l = parts(g1[block, i].reshape(256, 128))
            b1h[pl.ds(at, 256), block * 128 : block * 128 + 128] = h
            b1l[pl.ds(at, 256), block * 128 : block * 128 + 128] = l
        return 0

    lax.fori_loop(0, 4, unpack_first, 0)

    def mid_body(i, _):
        at = pl.multiple_of(i * 256, 256)
        value = three(nn, p1h[...], p1l[...], b1h[:, pl.ds(at, 256)], b1l[:, pl.ds(at, 256)])
        for k in range(2):
            own = value[:ROWS, k * 128 : k * 128 + 128]
            other = value[ROWS:, k * 128 : k * 128 + 128]
            zero = jnp.where(mine, own, other)
            one = jnp.where(mine, other, own)
            mid[4 * i + 2 * k] = jnp.where(lane < 64, zero, pltpu.roll(one, 64, 1))
            mid[4 * i + 2 * k + 1] = jnp.where(lane < 64, pltpu.roll(zero, 64, 1), one)
        return 0

    lax.fori_loop(0, 2, mid_body, 0)
    run(lines2)
    mid_rx[place.chip] = mid[place.chip]
    copy, mid_wait = place.group(mid_rx.at[0:7])
    for chip, device in chips:
        copy(mid.at[chip], mid_rx.at[place.chip], device)

    run(lines2, planes2)
    rows8 = lax.broadcasted_iota(jnp.int32, (16, 8, 128), 1)

    def unpack_second(i, _):
        at = pl.multiple_of(i * 128, 128)
        for block in range(4):
            tiles = g2[block, i].reshape(16, 2, 8, 128)
            even, odd = tiles[:, 0], tiles[:, 1]
            low = jnp.where(rows8 < 4, even, pltpu.roll(odd, 4, 1)).reshape(128, 128)
            high = jnp.where(rows8 < 4, pltpu.roll(even, 4, 1), odd).reshape(128, 128)
            for base, value in ((0, low), (HALF, high)):
                h, l = parts(value)
                lanes = slice(base + block * 128, base + block * 128 + 128)
                b2h[pl.ds(at, 128), lanes] = h
                b2l[pl.ds(at, 128), lanes] = l
        return 0

    lax.fori_loop(0, 4, unpack_second, 0)

    def z_body(i, _):
        at = pl.multiple_of(i * 256, 256)
        value = three(nt, ch[...], cl[...], b2h[pl.ds(at, 256), :], b2l[pl.ds(at, 256), :])
        z_own[:, pl.ds(at, 256)] = value[:ROWS]
        z_out[:, pl.ds(at, 256)] = value[ROWS:]
        return 0

    z_waits = []
    for i in range(2):
        z_body(i, 0)
        block = (slice(None), slice(i * 256, i * 256 + 256))
        z_waits.append(place.copy(z_out.at[block], z_rx.at[block], partner))
    def column_block(out, i, lh, ll, rh, rl):
        value = three(tn, lh, ll, rh, rl)
        for block in range(4):
            out[block, i] = value[:, block * 128 : block * 128 + 128].reshape(2, 4, 4, 8, 128)

    def stack_rows(src, out):
        def body(i, _):
            at = pl.multiple_of(i * 32, 32)
            h, l = parts(src[pl.ds(at, 32), :])
            out[pl.ds(at, 32), :] = h
            out[pl.ds(ROWS + at, 32), :] = l
            return 0

        lax.fori_loop(0, 4, body, 0)

    stack_rows(z_own, bmh)

    def back_body(i, _):
        value = folded(nt(bmh[...], hot2z[pl.ds(pl.multiple_of(i * 256, 256), 256), :HALF]))
        back[2 * i] = value[:, :128]
        back[2 * i + 1] = value[:, 128:]
        return 0

    lax.fori_loop(0, 4, back_body, 0)

    mid_wait()
    for chip in range(8):
        h, l = parts(mid_rx[chip])
        sph[:ROWS, chip * 128 : chip * 128 + 128] = h
        sph[ROWS:, chip * 128 : chip * 128 + 128] = l

    side = pl.multiple_of(core * HALF, HALF)
    a2_waits = []
    for i in range(4):
        lanes = slice(i * 256, i * 256 + 256)
        value = folded(nn(sph[...], hot2q[:, lanes]))
        a2_own[:, lanes] = value
        a2_waits.append(place.copy(a2_own.at[:, lanes], a2_rx.at[:, lanes], partner))
        a2h[:ROWS, lanes], a2l[:ROWS, lanes] = parts(value)
    done(z_waits)

    bit, pair = lax.rem(place.chip, 2), place.chip // 2
    copy, back_wait = place.group(back_rx.at[0:7])
    stack_rows(z_rx, bml)
    for turn in (1, 2, 3, 0):
        to = lax.rem(pair + turn, 4)
        value = folded(nt(bml[...], hot2z[pl.ds(pl.multiple_of(to * 256, 256), 256), HALF:]))
        back[2 * to] = back[2 * to] + value[:, :128]
        back[2 * to + 1] = back[2 * to + 1] + value[:, 128:]
        for half in (bit, 1 - bit) if turn else (1 - bit,):
            chip = to * 2 + half
            device = chip * 2 + core, lax.axis_index("gy")
            copy(back.at[chip], back_rx.at[place.chip], device)
    back_rx[place.chip] = back[place.chip]

    for i in range(4):
        lanes = slice(i * 256, i * 256 + 256)
        done(a2_waits[i : i + 1])
        a2h[ROWS:, lanes], a2l[ROWS:, lanes] = parts(a2_rx[:, lanes])
        column_block(s2, i, a2h[:, lanes], a2l[:, lanes], ch[:, pl.ds(side, HALF)], cl[:, pl.ds(side, HALF)])
    mark = place.used
    back2 = scatter_lines(place, s2, land2, *LINES_B)
    run(back2)

    place.sent(mark)
    back_wait()
    for pair in range(4):
        even, odd = back_rx[2 * pair], back_rx[2 * pair + 1]
        zero = jnp.where(lane < 64, even, pltpu.roll(odd, 64, 1))
        one = jnp.where(lane < 64, pltpu.roll(even, 64, 1), odd)
        for base, value in ((0, jnp.where(mine, zero, one)), (ROWS, jnp.where(mine, one, zero))):
            h, l = parts(value)
            bmh[base : base + ROWS, pair * 128 : pair * 128 + 128] = h
            bml[base : base + ROWS, pair * 128 : pair * 128 + 128] = l

    def first_body(i, _):
        at = pl.multiple_of(i * 256, 256)
        column_block(s1, i, p1h[:, pl.ds(at, 256)], p1l[:, pl.ds(at, 256)], bmh[...], bml[...])
        return 0

    lax.fori_loop(0, 4, first_body, 0)
    back1, back1w = scatter_lines(place, s1, land1, *LINES_A), scatter_planes(place, s1, land1w, *PLANES_A)
    run(back1, back1w)

    def y_body(i, _):
        at = pl.multiple_of(i * 256, 256)
        value = three(nt, bmh[...], bml[...], b1h[pl.ds(at, 256), :], b1l[pl.ds(at, 256), :])
        y_own[:, pl.ds(at, 256)] = value[:ROWS]
        y_out[:, pl.ds(at, 256)] = value[ROWS:]
        return 0

    lax.fori_loop(0, 4, y_body, 0)
    y_wait = place.copy(y_out, y_rx, partner)
    run(back2)
    run(back1)
    y_wait()

    def sum_rows(i, _):
        at = pl.multiple_of(i * 32, 32)
        h, l = parts(y_own[pl.ds(at, 32), :] + y_rx[pl.ds(at, 32), :])
        p1h[pl.ds(at, 32), :] = h
        p1h[pl.ds(ROWS + at, 32), :] = l
        return 0

    lax.fori_loop(0, ROWS // 32, sum_rows, 0)

    def grad_stem_body(i, _):
        at = pl.multiple_of(i * 256, 256)
        stem_rx[:, pl.ds(at, 256)] = folded(nt(p1h[...], hot1[pl.ds(at, 256), :]))
        return 0

    lax.fori_loop(0, 4, grad_stem_body, 0)
    result = pltpu.make_async_copy(stem_rx, grad_stem, local.at[2])
    result.start()
    mark = place.used
    run(back2, back1, back2, back1w, back1)
    place.sent(mark)
    run(back2)
    factor = 1.0 / (32768.0**0.5)
    ends[2] = s2[here].reshape(4, 8, 128) * factor
    second_done = place.copy(ends.at[2], ends.at[3], partner)

    def own_rows(tile):
        return jnp.where(mine, tile[:4], tile[4:])

    second_done()
    for block in range(4):
        own, other = own_rows(ends[2, block]), own_rows(ends[3, block])
        grad_second[:, block * 128 : block * 128 + 128] = jnp.where(mine, own, other)
        grad_second[:, HALF + block * 128 : HALF + block * 128 + 128] = jnp.where(mine, other, own)
    run(back1, back1w)
    ends[0] = s1[here].reshape(4, 8, 128) * factor
    first_done = place.copy(ends.at[0], ends.at[1], partner)
    first_done()
    for block in range(4):
        own, other = own_rows(ends[0, block]), own_rows(ends[1, block])
        left, right = halves(jnp.where(mine, own, other), jnp.where(mine, other, own), lane4)
        grad_first[:, block * 256 : block * 256 + 128] = left
        grad_first[:, block * 256 + 128 : block * 256 + 256] = right
    place.sent()
    result.wait()


def scratch_shapes():
    f32, b16 = (lambda *s: pltpu.VMEM(s, F32)), (lambda *s: pltpu.VMEM(s, BF16))
    shapes = [pltpu.SemaphoreType.DMA((GROUPS,)), pltpu.SemaphoreType.DMA((GROUPS,)), pltpu.SemaphoreType.DMA((3,))]
    field = (4, 4, 2, 4, 4, 8, 128)
    shapes += [f32(ROWS, WIDTH), f32(ROWS, WIDTH), f32(8, 128), f32(8, 128), f32(8, 128)]
    shapes += [f32(2, 4, 1, 1, 1, 1, 8, 128), f32(4, 4, 8, 128)]
    shapes += [f32(*field), f32(*field), f32(4, 1, 1, 1, 1, 8, 128), f32(ROWS, WIDTH), f32(ROWS, WIDTH)]
    shapes += [b16(WIDTH, WIDTH)] * 3
    shapes += [b16(2 * ROWS, WIDTH)] * 4 + [b16(WIDTH, HALF)] * 2 + [b16(HALF, WIDTH)] * 2
    shapes += [f32(ROWS, HALF)] * 3
    shapes += [f32(8, ROWS, 128)] * 4
    shapes += [b16(2 * ROWS, HALF)] * 2 + [b16(2 * ROWS, WIDTH)] * 2
    shapes += [f32(ROWS, WIDTH)] * 5 + [b16(2 * ROWS, WIDTH)] * 2
    shapes += [f32(*field)] * 2
    for dims in (line_landings(LINES_A[1]), plane_landings(PLANES_A[1]), line_landings(LINES_B[1])):
        shapes += [f32(*dim) for dim in dims]
    return shapes


def on_device(stem_first, cotangent, branch_first, branch_second, bond_first, bond_second):
    vmem, anywhere = pl.BlockSpec(memory_space=pltpu.VMEM), pl.BlockSpec(memory_space=pl.ANY)
    grad_stem, grad_first, grad_second = pl.pallas_call(
        kernel,
        out_shape=(
            jax.ShapeDtypeStruct((ROWS, WIDTH), F32),
            jax.ShapeDtypeStruct((4, WIDTH), F32),
            jax.ShapeDtypeStruct((4, WIDTH), F32),
        ),
        in_specs=[anywhere, anywhere] + [vmem] * 4,
        out_specs=(anywhere, vmem, vmem),
        scratch_shapes=scratch_shapes(),
        compiler_params=pltpu.CompilerParams(
            collective_id=0, has_side_effects=True, vmem_limit_bytes=60 * 2**20
        ),
    )(
        stem_first.reshape(ROWS, WIDTH),
        cotangent.reshape(ROWS, WIDTH),
        branch_first,
        branch_second,
        bond_first.reshape(8, 128),
        bond_second.reshape(8, 128),
    )
    return grad_stem.reshape(1, ROWS, WIDTH), grad_first, grad_second


def solution(mesh):
    return jax.shard_map(
        on_device,
        mesh=mesh,
        in_specs=(
            P("gx", "gy", None),
            P("gx", "gy", None),
            P(("gx", "gy"), None),
            P(("gx", "gy"), None),
            P(),
            P(),
        ),
        out_specs=(P("gx", "gy", None), P(("gx", "gy"), None), P(("gx", "gy"), None)),
        check_vma=False,
    )
```

```python
import jax
import jax.numpy as jnp
from jax import lax
from jax.experimental import pallas as pl
from jax.experimental.pallas import tpu as pltpu
from jax.sharding import PartitionSpec as P

MESH = pl.DeviceIdType.MESH
SIZE = {"x": 4, "y": 4, "z": 8}
DIM = {"x": 1, "y": 3, "z": 4}
ROWS = 128
WIDTH = 1024
HALF = 512
F32 = jnp.float32
BF16 = jnp.bfloat16

LINES_A, PLANES_A, LINES_B = (0, 3), (3, 1), (0, 4)
GROUPS = 56
PARTS = ((0, "y", "x"), (1, "x", "y"))


def dot(left, right, over):
    return lax.dot_general(left, right, (over, ((), ())), preferred_element_type=F32)


def nn(left, right):
    return dot(left, right, ((1,), (0,)))


def nt(left, right):
    return dot(left, right, ((1,), (1,)))


def tn(left, right):
    return dot(left, right, ((0,), (0,)))


def three(form, lhi, llo, rhi, rlo):
    return form(lhi, rhi) + (form(lhi, rlo) + form(llo, rhi))


def parts(value):
    high = value.astype(BF16)
    return high, (value - high.astype(F32)).astype(BF16)


class Place:
    def __init__(self, send, recv):
        gx, gy = lax.axis_index("gx"), lax.axis_index("gy")
        self.core = lax.rem(gx, 2)
        self.low = lax.rem(gx // 2, 2)
        self.at = {"x": gx // 4, "y": gy // 4, "z": lax.rem(gy, 4) * 2 + self.low}
        self.chip = gx // 2
        self.send, self.recv = send, recv
        self.used = 0
        self.drained = 0
        self.open = []

    def device(self, core=None, **where):
        spot = {**self.at, **where}
        core = self.core if core is None else core
        gx = (spot["x"] * 2 + lax.rem(spot["z"], 2)) * 2 + core
        return gx, spot["y"] * 4 + spot["z"] // 2

    def step(self, axis, by):
        return lax.rem(self.at[axis] + (by + SIZE[axis]), SIZE[axis])

    def neighbour(self, axis, by):
        return self.device(**{axis: self.step(axis, by)})

    def partner(self):
        return self.device(core=1 - self.core)

    def transfer(self, src, dst, slot, device):
        return pltpu.make_async_remote_copy(
            src_ref=src,
            dst_ref=dst,
            send_sem=self.send.at[slot],
            recv_sem=self.recv.at[slot],
            device_id=device,
            device_id_type=MESH,
        )

    def group(self, whole):
        slot = self.used
        self.used += 1
        together = self.transfer(whole, whole, slot, self.partner())
        self.open.append(together)

        def copy(src, dst, device):
            self.transfer(src, dst, slot, device).start()

        return copy, together.wait_recv

    def copy(self, src, dst, device):
        copy, wait = self.group(dst)
        copy(src, dst, device)
        return wait

    def sent(self, count=None):
        count = self.used if count is None else count
        for out in self.open[self.drained : count]:
            out.wait_send()
        self.drained = max(self.drained, count)


def view(block, count, spot, cut=None):
    index = [slice(block, block + count)] + [slice(None)] * 6
    for axis, value in spot.items():
        if axis == "z":
            index[2], index[4] = pl.ds(lax.rem(value, 2), 1), pl.ds(value // 2, 1)
        elif axis == "part":
            index[4] = slice(2 * value, 2 * value + 2)
        else:
            index[DIM[axis]] = pl.ds(value, 1)
    if cut is not None:
        name, which = cut
        index[DIM[name]] = slice(which * 2, which * 2 + 2)
    return tuple(index)


def hops():
    return [(dx, dy) for dx in range(4) for dy in range(4) if dx or dy]


def done(waits):
    for wait in waits:
        wait()


def spread(place, buffer, block, count, axis, rest, whole):
    mine = buffer.at[view(block, count, {**rest, axis: place.at[axis]})]
    copy, wait = place.group(whole)
    for by in range(1, SIZE[axis]):
        copy(mine, mine, place.neighbour(axis, by))
    return wait


def gather_planes(place, buffer, sizes, block, count):
    mine = buffer.at[view(block, count, place.at)]
    copy, wait = place.group(sizes[1])
    for dx, dy in hops():
        copy(mine, mine, place.device(x=place.step("x", dx), y=place.step("y", dy)))
    yield
    wait()
    wait = spread(place, buffer, block, count, "z", {}, sizes[0])
    yield
    wait()
    yield


def gather_lines(place, buffer, sizes, block, count):
    wait = spread(place, buffer, block, count, "z", {"x": place.at["x"], "y": place.at["y"]}, sizes[0])
    yield
    wait()
    both = buffer.at[block : block + count, 0:1, :, 0:1]
    near_groups = [place.group(both) for _ in range(3)]
    ahead = {line: place.group(both) for line in range(4)}
    last, last_wait = place.group(buffer.at[block : block + count, 0:2])

    def send(copy, part, near, far, line, sign, tick):
        spot = {"part": part, near: place.step(near, -line), far: place.step(far, -sign * tick)}
        out = buffer.at[view(block, count, spot)]
        copy(out, out, place.neighbour(far, sign))

    def ring(line, sign):
        for part in PARTS:
            send(ahead[line][0], *part, line, sign, 0)
            send(last, *part, line, -sign, 0)

    for part, near, far in PARTS:
        mine = buffer.at[view(block, count, {"part": part, near: place.at[near], far: place.at[far]})]
        for by in range(1, 4):
            near_groups[by - 1][0](mine, mine, place.neighbour(near, by))
    ring(0, 1)
    yield
    order = ((1, -1), (3, 1), (2, -1))
    for line, sign in order:
        near_groups[line - 1][1]()
        ring(line, sign)
    yield
    for line, sign in ((0, 1), *order):
        ahead[line][1]()
        for part in PARTS:
            send(last, *part, line, sign, 1)
    yield
    last_wait()
    yield


def line_landings(count):
    shapes = [(7, count, 1, 1, 1, 1, 8, 128)]
    for _ in PARTS:
        shapes += [(12, count, 1, 2, 1, 2, 8, 128), (3, count, 1, 2, 1, 2, 8, 128)]
    return shapes


def plane_landings(count):
    return [(7, count, 4, 1, 4, 1, 8, 128), (15, count, 1, 1, 1, 1, 8, 128)]


def collect(buffer, where, landing):
    total = buffer[where]
    for slot in range(landing.shape[0]):
        total = total + landing[slot]
    buffer[where] = total


def deliver(place, buffer, block, count, axis, rest, landing):
    copy, wait = place.group(landing)
    for by in range(1, SIZE[axis]):
        src = buffer.at[view(block, count, {**rest, axis: place.step(axis, by)})]
        copy(src, landing.at[by - 1], place.neighbour(axis, by))
    return wait


def scatter_planes(place, buffer, landings, block, count):
    wait = deliver(place, buffer, block, count, "z", {}, landings[0])
    yield
    wait()
    collect(buffer, view(block, count, {"z": place.at["z"]}), landings[0])
    copy, wait = place.group(landings[1])
    for slot, (dx, dy) in enumerate(hops()):
        spot = {"x": place.step("x", dx), "y": place.step("y", dy)}
        src = buffer.at[view(block, count, {**spot, "z": place.at["z"]})]
        copy(src, landings[1].at[slot], place.device(**spot))
    yield
    wait()
    collect(buffer, view(block, count, place.at), landings[1])
    yield


def scatter_lines(place, buffer, landings, block, count):
    last, rings, nears = landings[0], landings[1::2], landings[2::2]
    lines = ((2, 1), (1, -1), (0, 1), (3, -1))
    ahead = {line: place.group(rings[0].at[0:2]) for line in range(4)}
    close = {line: place.group(rings[0].at[0:4]) for line in range(4)}

    def piece(part, near, far, line, by):
        return view(block, count, {"part": part, near: place.step(near, line), far: place.step(far, by)})

    def send(copy, part, near, far, line, sign, distance, slot):
        there = rings[part].at[line * 3 + slot]
        copy(buffer.at[piece(part, near, far, line, sign * distance)], there, place.neighbour(far, sign))

    for line, sign in lines:
        for part in PARTS:
            send(ahead[line][0], *part, line, sign, 2, 0)
    for line, sign in lines:
        for part in PARTS:
            send(close[line][0], *part, line, -sign, 1, 2)
    yield
    for line, sign in lines:
        ahead[line][1]()
        for part in PARTS:
            where = piece(*part, line, sign)
            buffer[where] = buffer[where] + rings[part[0]][line * 3]
            send(close[line][0], *part, line, sign, 1, 1)
    yield
    copy, wait = place.group(rings[0].at[0:6])
    for line in (2, 1, 3, 0):
        close[line][1]()
        for part in PARTS:
            where = piece(*part, line, 0)
            which, near, far = part
            buffer[where] = buffer[where] + (rings[which][line * 3 + 1] + rings[which][line * 3 + 2])
            if line:
                copy(buffer.at[where], nears[which].at[line - 1], place.neighbour(near, line))
    yield
    wait()
    spot = {"x": place.at["x"], "y": place.at["y"]}
    for part, _, _ in PARTS:
        collect(buffer, view(block, count, {**spot, "part": part}), nears[part])
    wait = deliver(place, buffer, block, count, "z", spot, last)
    yield
    wait()
    collect(buffer, view(block, count, place.at), last)
    yield


def run(*streams):
    for stream in streams:
        next(stream)


def kernel(
    stem_hbm, cotan_hbm, branch_first, branch_second, bond_first, bond_second,
    grad_stem, grad_first, grad_second,
    *scratch,
):
    scratch = list(scratch)

    def take(n=None):
        if n is None:
            return scratch.pop(0)
        return [scratch.pop(0) for _ in range(n)]

    send, recv, local = take(3)
    stem_in, cotan_in, bq1, bq2, bz2, first_in, ends = take(7)
    g1, g2, rx1, stem_rx, cotan_rx = take(5)
    hot1, hot2q, hot2z = take(3)
    p1h, p1l, ch, cl, b1h, b1l, b2h, b2l = take(8)
    z_own, z_out, z_rx = take(3)
    back, back_rx, mid, mid_rx = take(4)
    bmh, bml, sph, spl = take(4)
    y_own, y_out, y_rx, a2_own, a2_rx = take(5)
    a2h, a2l = take(2)
    s1, s2 = take(2)
    land1, land1w, land2 = take(5), take(2), take(5)

    place = Place(send, recv)
    core = place.core
    mine = core == 0

    barrier = pltpu.get_barrier_semaphore()
    chips = []
    for hop in range(1, 8):
        chip = lax.rem(place.chip + hop, 8)
        chips.append((chip, (chip * 2 + core, lax.axis_index("gy"))))
    peers = [place.partner()]
    for axis in "xyz":
        peers += [place.neighbour(axis, by) for by in range(1, SIZE[axis])]
    beside = place.at["z"] + 1 - 2 * place.low
    peers += [place.device(x=place.step("x", by), z=beside) for by in range(1, 4)]
    peers += [place.device(x=place.step("x", dx), y=place.step("y", dy)) for dx, dy in hops() if dx and dy]
    for peer in peers:
        pl.semaphore_signal(barrier, inc=1, device_id=peer, device_id_type=MESH)

    stem_load = pltpu.make_async_copy(stem_hbm, stem_in, local.at[0])
    stem_load.start()
    cotan_load = pltpu.make_async_copy(cotan_hbm, cotan_in, local.at[1])
    cotan_load.start()

    here = view(0, 4, place.at)
    lane4 = lax.broadcasted_iota(jnp.int32, (4, 128), 1)

    def folded(value):
        return value[:ROWS] + value[ROWS:]

    def halves(even, odd, lanes):
        return jnp.where(lanes < 64, even, pltpu.roll(odd, 64, 1)), jnp.where(lanes < 64, pltpu.roll(even, 64, 1), odd)

    for block in range(4):
        lanes = slice(block * 128, block * 128 + 128)
        tile = jnp.concatenate([branch_second[:, lanes], branch_second[:, HALF + block * 128 : HALF + block * 128 + 128]], 0)
        g2[view(block, 1, place.at)] = tile.reshape(1, 1, 1, 1, 1, 8, 128)
        pair = halves(
            branch_first[:, block * 256 : block * 256 + 128], branch_first[:, block * 256 + 128 : block * 256 + 256], lane4
        )
        for side in range(2):
            none = jnp.zeros_like(pair[side])
            tile = jnp.where(mine, jnp.concatenate([pair[side], none], 0), jnp.concatenate([none, pair[side]], 0))
            first_in[side, block] = tile.reshape(1, 1, 1, 1, 8, 128)

    def digit(row, lanes):
        return jnp.where(row == lax.rem(lanes // 4, 2) * 64 + lanes // 8 * 4 + lax.rem(lanes, 4), 1.0, 0.0).astype(BF16)

    shuffle = digit(lax.broadcasted_iota(jnp.int32, (128, 128), 0), lax.broadcasted_iota(jnp.int32, (128, 128), 1))
    for bond, out in ((bond_first, bq1), (bond_second, bq2)):
        value = bond[...]
        high = (value // 32).astype(F32).astype(BF16)
        low = lax.rem(value, 32).astype(F32).astype(BF16)
        out[...] = nn(high, shuffle) * 32.0 + nn(low, shuffle)
    lane1 = lax.broadcasted_iota(jnp.int32, (1, 128), 1)
    for pair in range(4):
        zero, one = halves(bond_second[2 * pair : 2 * pair + 1, :], bond_second[2 * pair + 1 : 2 * pair + 2, :], lane1)
        bz2[pair : pair + 1, :] = jnp.where(mine, zero, one).astype(F32)
        bz2[pair + 4 : pair + 5, :] = jnp.where(mine, one, zero).astype(F32)

    pl.semaphore_wait(barrier, len(peers))

    partner = place.partner()
    first_wait = place.copy(first_in.at[1 - core], rx1, partner)
    lines1 = gather_lines(place, g1, land2, *LINES_B)
    lines2, planes2 = gather_lines(place, g2, land1, *LINES_A), gather_planes(place, g2, land1w, *PLANES_A)
    run(planes2)
    first_wait()
    g1[here] = first_in[core] + rx1[...]
    run(lines1)
    stem_load.wait()
    cotan_load.wait()
    stem_wait = place.copy(stem_in, stem_rx, partner)
    cotan_wait = place.copy(cotan_in, cotan_rx, partner)

    def build(hot, bond):
        def body(i, _):
            at = pl.multiple_of(i * 64, 64)
            rows = (lax.broadcasted_iota(jnp.int32, (64, 128), 0) + at).astype(F32)
            for group in range(8):
                hit = rows == bond[group : group + 1, :]
                hot[pl.ds(at, 64), group * 128 : group * 128 + 128] = jnp.where(hit, 1.0, 0.0).astype(BF16)
            return 0

        lax.fori_loop(0, WIDTH // 64, body, 0)

    def split_rows(src, high, low, base):
        def body(i, _):
            at = pl.multiple_of(i * 32, 32)
            h, l = parts(src[pl.ds(at, 32), :])
            high[pl.ds(base + at, 32), :] = h
            low[pl.ds(base + at, 32), :] = l
            return 0

        lax.fori_loop(0, src.shape[0] // 32, body, 0)

    build(hot1, bq1)
    split_rows(stem_in, sph, spl, 0)
    stem_wait()
    split_rows(stem_rx, sph, spl, ROWS)

    def permute_stem(i, _):
        at = pl.multiple_of(i * 256, 256)
        hot = hot1[:, pl.ds(at, 256)]
        p1h[:, pl.ds(at, 256)] = nn(sph[...], hot).astype(BF16)
        p1l[:, pl.ds(at, 256)] = nn(spl[...], hot).astype(BF16)
        return 0

    lax.fori_loop(0, 4, permute_stem, 0)
    split_rows(cotan_in, ch, cl, 0)
    cotan_wait()
    split_rows(cotan_rx, ch, cl, ROWS)
    run(lines1, lines2, planes2)
    build(hot2q, bq2)
    run(lines1, lines2)
    build(hot2z, bz2)
    run(lines1, lines2)

    lane = lax.broadcasted_iota(jnp.int32, (ROWS, 128), 1)

    run(lines2, lines1)

    def unpack_first(i, _):
        at = pl.multiple_of(i * 256, 256)
        for block in range(4):
            h, l = parts(g1[block, i].reshape(256, 128))
            b1h[pl.ds(at, 256), block * 128 : block * 128 + 128] = h
            b1l[pl.ds(at, 256), block * 128 : block * 128 + 128] = l
        return 0

    lax.fori_loop(0, 4, unpack_first, 0)

    def mid_body(i, _):
        at = pl.multiple_of(i * 256, 256)
        value = three(nn, p1h[...], p1l[...], b1h[:, pl.ds(at, 256)], b1l[:, pl.ds(at, 256)])
        for k in range(2):
            own = value[:ROWS, k * 128 : k * 128 + 128]
            other = value[ROWS:, k * 128 : k * 128 + 128]
            zero = jnp.where(mine, own, other)
            one = jnp.where(mine, other, own)
            mid[4 * i + 2 * k] = jnp.where(lane < 64, zero, pltpu.roll(one, 64, 1))
            mid[4 * i + 2 * k + 1] = jnp.where(lane < 64, pltpu.roll(zero, 64, 1), one)
        return 0

    lax.fori_loop(0, 2, mid_body, 0)
    mid_rx[place.chip] = mid[place.chip]
    copy, mid_wait = place.group(mid_rx.at[0:7])
    for chip, device in chips:
        copy(mid.at[chip], mid_rx.at[place.chip], device)

    run(lines2, planes2)
    rows8 = lax.broadcasted_iota(jnp.int32, (16, 8, 128), 1)

    def unpack_second(i, _):
        at = pl.multiple_of(i * 128, 128)
        for block in range(4):
            tiles = g2[block, i].reshape(16, 2, 8, 128)
            even, odd = tiles[:, 0], tiles[:, 1]
            low = jnp.where(rows8 < 4, even, pltpu.roll(odd, 4, 1)).reshape(128, 128)
            high = jnp.where(rows8 < 4, pltpu.roll(even, 4, 1), odd).reshape(128, 128)
            for base, value in ((0, low), (HALF, high)):
                h, l = parts(value)
                lanes = slice(base + block * 128, base + block * 128 + 128)
                b2h[pl.ds(at, 128), lanes] = h
                b2l[pl.ds(at, 128), lanes] = l
        return 0

    lax.fori_loop(0, 4, unpack_second, 0)

    def z_body(i, _):
        at = pl.multiple_of(i * 256, 256)
        value = three(nt, ch[...], cl[...], b2h[pl.ds(at, 256), :], b2l[pl.ds(at, 256), :])
        z_own[:, pl.ds(at, 256)] = value[:ROWS]
        z_out[:, pl.ds(at, 256)] = value[ROWS:]
        return 0

    z_waits = []
    for i in range(2):
        z_body(i, 0)
        block = (slice(None), slice(i * 256, i * 256 + 256))
        z_waits.append(place.copy(z_out.at[block], z_rx.at[block], partner))
    def column_block(out, i, lh, ll, rh, rl):
        value = three(tn, lh, ll, rh, rl)
        for block in range(4):
            out[block, i] = value[:, block * 128 : block * 128 + 128].reshape(2, 4, 4, 8, 128)

    def stack_rows(src, out):
        def body(i, _):
            at = pl.multiple_of(i * 32, 32)
            h, l = parts(src[pl.ds(at, 32), :])
            out[pl.ds(at, 32), :] = h
            out[pl.ds(ROWS + at, 32), :] = l
            return 0

        lax.fori_loop(0, 4, body, 0)

    stack_rows(z_own, bmh)

    def back_body(i, _):
        value = folded(nt(bmh[...], hot2z[pl.ds(pl.multiple_of(i * 256, 256), 256), :HALF]))
        back[2 * i] = value[:, :128]
        back[2 * i + 1] = value[:, 128:]
        return 0

    lax.fori_loop(0, 4, back_body, 0)

    mid_wait()
    for chip in range(8):
        h, l = parts(mid_rx[chip])
        sph[:ROWS, chip * 128 : chip * 128 + 128] = h
        sph[ROWS:, chip * 128 : chip * 128 + 128] = l

    side = pl.multiple_of(core * HALF, HALF)
    a2_waits = []
    for i in range(4):
        lanes = slice(i * 256, i * 256 + 256)
        value = folded(nn(sph[...], hot2q[:, lanes]))
        a2_own[:, lanes] = value
        a2_waits.append(place.copy(a2_own.at[:, lanes], a2_rx.at[:, lanes], partner))
        a2h[:ROWS, lanes], a2l[:ROWS, lanes] = parts(value)
    done(z_waits)

    bit, pair = lax.rem(place.chip, 2), place.chip // 2
    copy, back_wait = place.group(back_rx.at[0:7])
    stack_rows(z_rx, bml)
    for turn in (1, 2, 3, 0):
        to = lax.rem(pair + turn, 4)
        value = folded(nt(bml[...], hot2z[pl.ds(pl.multiple_of(to * 256, 256), 256), HALF:]))
        back[2 * to] = back[2 * to] + value[:, :128]
        back[2 * to + 1] = back[2 * to + 1] + value[:, 128:]
        for half in (bit, 1 - bit) if turn else (1 - bit,):
            chip = to * 2 + half
            device = chip * 2 + core, lax.axis_index("gy")
            copy(back.at[chip], back_rx.at[place.chip], device)
    back_rx[place.chip] = back[place.chip]

    for i in range(4):
        lanes = slice(i * 256, i * 256 + 256)
        done(a2_waits[i : i + 1])
        a2h[ROWS:, lanes], a2l[ROWS:, lanes] = parts(a2_rx[:, lanes])
        column_block(s2, i, a2h[:, lanes], a2l[:, lanes], ch[:, pl.ds(side, HALF)], cl[:, pl.ds(side, HALF)])
    mark = place.used
    back2 = scatter_lines(place, s2, land2, *LINES_B)
    run(back2)

    place.sent(mark)
    back_wait()
    for pair in range(4):
        even, odd = back_rx[2 * pair], back_rx[2 * pair + 1]
        zero = jnp.where(lane < 64, even, pltpu.roll(odd, 64, 1))
        one = jnp.where(lane < 64, pltpu.roll(even, 64, 1), odd)
        for base, value in ((0, jnp.where(mine, zero, one)), (ROWS, jnp.where(mine, one, zero))):
            h, l = parts(value)
            bmh[base : base + ROWS, pair * 128 : pair * 128 + 128] = h
            bml[base : base + ROWS, pair * 128 : pair * 128 + 128] = l

    def first_body(i, _):
        at = pl.multiple_of(i * 256, 256)
        column_block(s1, i, p1h[:, pl.ds(at, 256)], p1l[:, pl.ds(at, 256)], bmh[...], bml[...])
        return 0

    lax.fori_loop(0, 4, first_body, 0)
    back1, back1w = scatter_lines(place, s1, land1, *LINES_A), scatter_planes(place, s1, land1w, *PLANES_A)
    run(back1, back1w)

    def y_body(i, _):
        at = pl.multiple_of(i * 256, 256)
        value = three(nt, bmh[...], bml[...], b1h[pl.ds(at, 256), :], b1l[pl.ds(at, 256), :])
        y_own[:, pl.ds(at, 256)] = value[:ROWS]
        y_out[:, pl.ds(at, 256)] = value[ROWS:]
        return 0

    lax.fori_loop(0, 4, y_body, 0)
    y_wait = place.copy(y_out, y_rx, partner)
    run(back2)
    run(back1)
    y_wait()

    def sum_rows(i, _):
        at = pl.multiple_of(i * 32, 32)
        h, l = parts(y_own[pl.ds(at, 32), :] + y_rx[pl.ds(at, 32), :])
        p1h[pl.ds(at, 32), :] = h
        p1h[pl.ds(ROWS + at, 32), :] = l
        return 0

    lax.fori_loop(0, ROWS // 32, sum_rows, 0)

    def grad_stem_body(i, _):
        at = pl.multiple_of(i * 256, 256)
        stem_rx[:, pl.ds(at, 256)] = folded(nt(p1h[...], hot1[pl.ds(at, 256), :]))
        return 0

    lax.fori_loop(0, 4, grad_stem_body, 0)
    result = pltpu.make_async_copy(stem_rx, grad_stem, local.at[2])
    result.start()
    mark = place.used
    run(back2, back1, back2, back1w, back1)
    place.sent(mark)
    run(back2)
    factor = 1.0 / (32768.0**0.5)
    ends[2] = s2[here].reshape(4, 8, 128) * factor
    second_done = place.copy(ends.at[2], ends.at[3], partner)

    def own_rows(tile):
        return jnp.where(mine, tile[:4], tile[4:])

    second_done()
    for block in range(4):
        own, other = own_rows(ends[2, block]), own_rows(ends[3, block])
        grad_second[:, block * 128 : block * 128 + 128] = jnp.where(mine, own, other)
        grad_second[:, HALF + block * 128 : HALF + block * 128 + 128] = jnp.where(mine, other, own)
    run(back1, back1w)
    ends[0] = s1[here].reshape(4, 8, 128) * factor
    first_done = place.copy(ends.at[0], ends.at[1], partner)
    first_done()
    for block in range(4):
        own, other = own_rows(ends[0, block]), own_rows(ends[1, block])
        left, right = halves(jnp.where(mine, own, other), jnp.where(mine, other, own), lane4)
        grad_first[:, block * 256 : block * 256 + 128] = left
        grad_first[:, block * 256 + 128 : block * 256 + 256] = right
    place.sent()
    result.wait()


def scratch_shapes():
    f32, b16 = (lambda *s: pltpu.VMEM(s, F32)), (lambda *s: pltpu.VMEM(s, BF16))
    shapes = [pltpu.SemaphoreType.DMA((GROUPS,)), pltpu.SemaphoreType.DMA((GROUPS,)), pltpu.SemaphoreType.DMA((3,))]
    field = (4, 4, 2, 4, 4, 8, 128)
    shapes += [f32(ROWS, WIDTH), f32(ROWS, WIDTH), f32(8, 128), f32(8, 128), f32(8, 128)]
    shapes += [f32(2, 4, 1, 1, 1, 1, 8, 128), f32(4, 4, 8, 128)]
    shapes += [f32(*field), f32(*field), f32(4, 1, 1, 1, 1, 8, 128), f32(ROWS, WIDTH), f32(ROWS, WIDTH)]
    shapes += [b16(WIDTH, WIDTH)] * 3
    shapes += [b16(2 * ROWS, WIDTH)] * 4 + [b16(WIDTH, HALF)] * 2 + [b16(HALF, WIDTH)] * 2
    shapes += [f32(ROWS, HALF)] * 3
    shapes += [f32(8, ROWS, 128)] * 4
    shapes += [b16(2 * ROWS, HALF)] * 2 + [b16(2 * ROWS, WIDTH)] * 2
    shapes += [f32(ROWS, WIDTH)] * 5 + [b16(2 * ROWS, WIDTH)] * 2
    shapes += [f32(*field)] * 2
    for dims in (line_landings(LINES_A[1]), plane_landings(PLANES_A[1]), line_landings(LINES_B[1])):
        shapes += [f32(*dim) for dim in dims]
    return shapes


def on_device(stem_first, cotangent, branch_first, branch_second, bond_first, bond_second):
    vmem, anywhere = pl.BlockSpec(memory_space=pltpu.VMEM), pl.BlockSpec(memory_space=pl.ANY)
    grad_stem, grad_first, grad_second = pl.pallas_call(
        kernel,
        out_shape=(
            jax.ShapeDtypeStruct((ROWS, WIDTH), F32),
            jax.ShapeDtypeStruct((4, WIDTH), F32),
            jax.ShapeDtypeStruct((4, WIDTH), F32),
        ),
        in_specs=[anywhere, anywhere] + [vmem] * 4,
        out_specs=(anywhere, vmem, vmem),
        scratch_shapes=scratch_shapes(),
        compiler_params=pltpu.CompilerParams(
            collective_id=0, has_side_effects=True, vmem_limit_bytes=60 * 2**20
        ),
    )(
        stem_first.reshape(ROWS, WIDTH),
        cotangent.reshape(ROWS, WIDTH),
        branch_first,
        branch_second,
        bond_first.reshape(8, 128),
        bond_second.reshape(8, 128),
    )
    return grad_stem.reshape(1, ROWS, WIDTH), grad_first, grad_second


def solution(mesh):
    return jax.shard_map(
        on_device,
        mesh=mesh,
        in_specs=(
            P("gx", "gy", None),
            P("gx", "gy", None),
            P(("gx", "gy"), None),
            P(("gx", "gy"), None),
            P(),
            P(),
        ),
        out_specs=(P("gx", "gy", None), P(("gx", "gy"), None), P(("gx", "gy"), None)),
        check_vma=False,
    )
```
